32 devices in a mesh: groups: 2 (over x), pen: 16 (over z, y, core).
Axes of the slice: x: 2, y: 2, z: 4, core: 2. Of those that a mesh axis runs over, the one named last changes fastest.
Arguments:
- point_feat: bfloat16 [64, 65536], P(None, ('groups', 'pen')), parts along dimension 1, may hold values from -6 to 6
- pair_kernel: bfloat16 [2048, 128, 128], P(('groups', 'pen')), parts along dimension 0, may hold values from -0.5 to 0.5
- pair_owner: int32 [2048, 1], P(('groups', 'pen')), parts along dimension 0, may hold values from 0 to 15; in each aligned block of 64 rows (0 to 63, 64 to 127, ...) at most 8 rows name the same one
- pair_block: int32 [2048], P(('groups', 'pen')), parts along dimension 0, may hold values from 0 to 255
- spec_weight: bfloat16 [2, 256, 16, 64, 128], P(None, 'pen'), may hold values from -3 to 3
- mlp_up: bfloat16 [2, 256, 64], replicated, may hold values from -0.75 to 0.75
- mlp_down: bfloat16 [2, 64, 256], replicated, may hold values from -0.375 to 0.375
Outputs:
- point_out: float32 [64, 65536], P(None, ('groups', 'pen')), parts along dimension 1
The draws below stay inside these ranges and needn't reach their ends.
There are 2 independent parts, one for each index of `groups`. The reference program is written for one: setup_inputs(seed, part) draws one part's arguments, and reference() takes and returns one part's arrays. A program takes and returns all parts, laid end to end along the dimension named above; an argument that names none is the same for every part. Nothing has to cross between parts.
Inputs may be any that keep to these rules, and one draw needn't show every extreme that they name: `pair_owner`: among the pairs of one device, no device is named more than 8 times.
All inputs are finite; a program needn't handle non-finite values.
Results may differ from the reference program's by a relative error of at most 0.0055.
Values may be sent and summed in bfloat16 or wider, within the bound.
A program may use at most 128 MiB of HBM per device.

```python
import math
import jax
import jax.numpy as jnp
import numpy as np
from jax import lax

C = 64
HID = 256
NX = 128
NY = 64
NZ = 64
MX = 16
MY = 16
MZ = 16
LAYERS = 2
BS = 128
NBR = 4
BLK_DEV = 16
CAP = 8
PAIRS = 1024
NPTS = 32768
GB_DEV = 256
N_PEN = 16


def set_ends(values, rng, least, top_value):
    extent = values.shape
    place = [jax.random.randint(jax.random.fold_in(rng, axis), (), 0, extent[axis]) for axis in range(len(extent))]
    values = values.at[tuple(place)].set(least)
    longest = extent.index(max(extent))
    place[longest] = (place[longest] + 1) % extent[longest]
    return values.at[tuple(place)].set(top_value)


def block_levels(stream_key, shape, pieces, low, top_value):
    def one(dim, shards_of):
        steps = jax.random.uniform(jax.random.fold_in(jax.random.fold_in(stream_key, 6), dim), (shards_of,), jnp.float32, low / len(pieces), top_value / len(pieces))
        return jnp.repeat(jnp.exp(steps), shape[dim] // shards_of).reshape((-1,) + (1,) * (len(shape) - dim - 1))

    factor_of = one(*pieces[0])
    for cut in pieces[1:]:
        factor_of = factor_of * one(*cut)
    return factor_of


def assign_block(stream_key, own, number, rows, amount, top, most, lean):
    ranking = jax.random.permutation(stream_key, amount)
    heavy_load, common = shares(amount, rows * top, most, lean, True), shares(amount, rows * top, most, lean, False)
    places = jnp.arange(amount)

    def named(lengths, turn):
        used = int((lengths > 0).sum())
        fixed = max(1, used // 4)
        passed = fixed + (places - fixed + turn * (used - fixed)) % max(1, amount - fixed)
        return jnp.zeros((amount,), jnp.int32).at[ranking[jnp.where(places < fixed, places, passed)]].set(jnp.asarray(lengths, jnp.int32))

    lengths = jnp.where(number % 4 == 0, named(heavy_load, number // 4), named(common, number - number // 4 - 1))
    mixed = jax.random.permutation(jax.random.fold_in(own, 3), amount)
    source_of, receiver = mixed[0:amount // 2 * 2:2], mixed[1:amount // 2 * 2:2]
    room = jnp.minimum(lengths[source_of] - 1, most - lengths[receiver]) // 2
    room = jnp.where((source_of == ranking[0]) | (receiver == ranking[0]) | (lengths[receiver] == 0), 0, jnp.maximum(room, 0))
    passed = jax.random.randint(jax.random.fold_in(own, 4), (amount // 2,), 0, 1 << 20) % (room + 1)
    lengths = lengths.at[source_of].add(-passed).at[receiver].add(passed)
    members = jnp.searchsorted(jnp.cumsum(lengths), jnp.arange(rows * top), side="right").astype(jnp.int32)
    table = members.reshape(top, rows).T
    table = table[jax.random.permutation(jax.random.fold_in(own, 1), rows)]
    turn = jax.random.randint(jax.random.fold_in(own, 2), (rows, 1), 0, top)
    return jnp.take_along_axis(table, (jnp.arange(top)[None, :] + turn) % top, axis=1)


def shares(number_of, total, limit, skew, full):
    portions = [(1 << 20) // math.isqrt(grade ** skew) + 1 for grade in range(1, number_of + 1)]
    largest = limit if full else min(limit, max(-(-total // number_of), total * portions[0] // sum(portions)))
    least = 1 if total - largest >= number_of - 1 else 0
    counts, spare = [largest] + [least] * (number_of - 1), total - largest - least * (number_of - 1)
    while spare > 0:
        movable = [i for i in range(1, number_of) if counts[i] < largest] or [i for i in range(1, number_of) if counts[i] < limit]
        mass, remaining = sum([portions[i] for i in movable]), spare
        for i in movable:
            addition = min(limit - counts[i], max(1, remaining * portions[i] // mass), spare)
            counts[i] = counts[i] + addition
            spare = spare - addition
    return np.array(counts)


def noise(key, dims, scale, most, shards=(), held_as=jnp.bfloat16):
    factor_of = block_levels(key, dims, shards, -0.22, 0.18) if shards else 1.0
    drawn = jax.random.normal(key, dims, jnp.float32) * scale * factor_of
    return jnp.minimum(jnp.maximum(drawn, -most), most).astype(held_as)


def setup_inputs(seed: int = 0, part: int = 0) -> dict:
    arg_keys = jax.random.split(jax.random.key(seed), 8)
    own_keys = jax.random.split(jax.random.fold_in(arg_keys[7], part), 8)
    point_feat = noise(own_keys[0], (C, NPTS), 1.0, 6.0, ((1, 16),))
    pair_kernel = noise(own_keys[1], (PAIRS, BS, BS), BS ** -0.5, 0.5, ((0, 16),))
    pair_owner_keys = jax.random.split(jax.random.fold_in(own_keys[2], 1), PAIRS // (BLK_DEV * NBR))
    pair_owner_turns = jax.random.permutation(jax.random.fold_in(own_keys[2], 3), PAIRS // (BLK_DEV * NBR))
    pair_owner = jax.vmap(lambda own, number: assign_block(jax.random.fold_in(own_keys[2], 2), own, number, BLK_DEV * NBR, N_PEN, 1, CAP, 2))(pair_owner_keys, pair_owner_turns).reshape((PAIRS, 1))
    pair_block = set_ends(jax.random.randint(own_keys[3], (PAIRS,), 0, GB_DEV), jax.random.fold_in(own_keys[3], 1), 0, GB_DEV - 1).astype(jnp.int32)
    spec_weight = noise(arg_keys[4], (LAYERS, MY * MZ, MX, C, 2 * C), (C // 16) ** -0.5, 3.0, ((1, 16),))
    mlp_up = noise(arg_keys[5], (LAYERS, HID, C), C ** -0.5, 0.75)
    mlp_down = noise(arg_keys[6], (LAYERS, C, HID), HID ** -0.5, 0.375)
    return dict(point_feat=point_feat, pair_kernel=pair_kernel, pair_owner=pair_owner, pair_block=pair_block, spec_weight=spec_weight, mlp_up=mlp_up, mlp_down=mlp_down)


HIGHEST = lax.Precision.HIGHEST


def yz_tables():
    mode_index = jnp.arange(MY * MZ, dtype=jnp.int32)
    wave_y = mode_index // MZ - MY // 2
    wave_z = mode_index % MZ
    cell_index = jnp.arange(NY * NZ, dtype=jnp.int32)
    row_y = cell_index // NZ
    row_z = cell_index % NZ
    phase_turns = jnp.mod(row_y[:, None] * wave_y[None, :], NY).astype(jnp.float32) / NY + jnp.mod(row_z[:, None] * wave_z[None, :], NZ).astype(jnp.float32) / NZ
    angle = 2.0 * math.pi * phase_turns
    forward_table = jnp.stack([jnp.cos(angle), -jnp.sin(angle)], axis=2).reshape(NY * NZ, 2 * MY * MZ)
    scaling = jnp.where(wave_z == 0, 1.0, 2.0).astype(jnp.float32) / (NX * NY * NZ)
    inverse_table = forward_table * jnp.repeat(scaling, 2)[None, :]
    return forward_table, inverse_table


def along_tables(positions):
    wave_number = jnp.arange(MX, dtype=jnp.int32) - MX // 2
    angle = 2.0 * math.pi * jnp.mod(wave_number[:, None] * positions[None, :], NX).astype(jnp.float32) / NX
    return jnp.cos(angle), jnp.sin(angle)


def spectral_part(grid_field, weights_now, forward_table, inverse_table):
    modes_all = MY * MZ
    planar = jnp.dot(grid_field.reshape(C * NX, NY * NZ), forward_table, precision=HIGHEST).reshape(C, NX, modes_all, 2)
    cosine_table, sine_table = along_tables(jnp.arange(NX, dtype=jnp.int32))
    part_real = planar[..., 0]
    part_imag = planar[..., 1]
    modes_real = jnp.einsum("jx,cxm->mjc", cosine_table, part_real, precision=HIGHEST) + jnp.einsum("jx,cxm->mjc", sine_table, part_imag, precision=HIGHEST)
    modes_imag = jnp.einsum("jx,cxm->mjc", cosine_table, part_imag, precision=HIGHEST) - jnp.einsum("jx,cxm->mjc", sine_table, part_real, precision=HIGHEST)
    weight_real = weights_now[..., :C].astype(jnp.float32)
    weight_imag = weights_now[..., C:].astype(jnp.float32)
    mixed_real = jnp.einsum("mjc,mjco->mjo", modes_real, weight_real, precision=HIGHEST) - jnp.einsum("mjc,mjco->mjo", modes_imag, weight_imag, precision=HIGHEST)
    mixed_imag = jnp.einsum("mjc,mjco->mjo", modes_real, weight_imag, precision=HIGHEST) + jnp.einsum("mjc,mjco->mjo", modes_imag, weight_real, precision=HIGHEST)
    back_real = jnp.einsum("jx,mjo->oxm", cosine_table, mixed_real, precision=HIGHEST) - jnp.einsum("jx,mjo->oxm", sine_table, mixed_imag, precision=HIGHEST)
    back_imag = jnp.einsum("jx,mjo->oxm", sine_table, mixed_real, precision=HIGHEST) + jnp.einsum("jx,mjo->oxm", cosine_table, mixed_imag, precision=HIGHEST)
    joined = jnp.stack([back_real, back_imag], axis=3).reshape(C * NX, 2 * modes_all)
    return jnp.dot(joined, inverse_table.T, precision=HIGHEST).reshape(C, NX, NY * NZ)


def channel_mlp(summed, weight_up, weight_down):
    def one_plane(values):
        rounded = values.astype(jnp.bfloat16)
        hidden = jnp.dot(weight_up, rounded, preferred_element_type=jnp.float32)
        active = jax.nn.gelu(hidden, approximate=True).astype(jnp.bfloat16)
        return values + jnp.dot(weight_down, active, preferred_element_type=jnp.float32)

    planes_first = jnp.moveaxis(summed, 1, 0)
    return jnp.moveaxis(lax.map(one_plane, planes_first), 0, 1)


def reference(point_feat, pair_kernel, pair_owner, pair_block, spec_weight, mlp_up, mlp_down):
    grid_total = NX * NY * NZ // BS
    target = pair_owner[:, 0] * GB_DEV + pair_block
    feature_blocks = point_feat.reshape(C, PAIRS // NBR, BS).transpose(1, 0, 2)
    pair_features = jnp.repeat(feature_blocks, NBR, axis=0)
    kernels_wide = pair_kernel.astype(jnp.float32)
    contrib = jnp.einsum("pci,pij->pcj", pair_features.astype(jnp.float32), kernels_wide)
    grid_blocks = jax.ops.segment_sum(contrib, target, num_segments=grid_total)
    grid_field = grid_blocks.transpose(1, 0, 2).reshape(C, NX, NY * NZ)
    forward_table, inverse_table = yz_tables()
    for number in range(LAYERS):
        spectral = spectral_part(grid_field, spec_weight[number], forward_table, inverse_table)
        summed = grid_field + spectral
        grid_field = channel_mlp(summed, mlp_up[number], mlp_down[number])
    grid_out = grid_field.astype(jnp.bfloat16).reshape(C, grid_total, BS).transpose(1, 0, 2)
    fetched = grid_out[target]
    back = jnp.einsum("pcj,pij->pci", fetched.astype(jnp.float32), kernels_wide)
    summed_back = back.reshape(PAIRS // NBR, NBR, C, BS).sum(axis=1)
    return summed_back.transpose(1, 0, 2).reshape(C, NPTS)
```

```python
import functools
import math

import jax
import jax.numpy as jnp
import numpy as np
from jax import lax
from jax.experimental import pallas as pl
from jax.experimental.pallas import tpu as pltpu
from jax.sharding import PartitionSpec as P

NX = 128
NY = 64
NZ = 64
MX = 16
MY = 16
MZ = 16
LAYERS = 2
NBR = 4
NOTE_ROWS = 16

F32 = jnp.float32
BF16 = jnp.bfloat16
VMEM = pl.BlockSpec(memory_space=pltpu.VMEM)
SMEM = pl.BlockSpec(memory_space=pltpu.SMEM)
NT = (((1,), (1,)), ((), ()))
TN = (((0,), (0,)), ((), ()))
MESH = pl.DeviceIdType.MESH
ANY = pl.BlockSpec(memory_space=pl.ANY)


def plane_table(devices, lanes):
    here = MY * MZ // devices
    row = np.arange(2 * MY * MZ)
    mode = row // (2 * here) * here + row % here
    imag = (row % (2 * here)) // here
    wave_y = mode // MZ - MY // 2
    wave_z = mode % MZ
    cell = np.arange(lanes)
    turns = np.mod(np.outer(wave_y, cell // NZ), NY) / NY + np.mod(np.outer(wave_z, cell % NZ), NZ) / NZ
    first = 2 * np.pi * turns + np.where(imag, np.pi / 2, 0.0)[:, None]
    tiles = NY * NZ // lanes
    step = 2 * np.pi * np.mod(np.outer(np.arange(tiles) * (lanes // NZ), wave_y), NY) / NY
    parts = [np.cos(first), np.sin(first), np.cos(step), np.sin(step)]
    cos0, sin0, cos_k, sin_k = lax.optimization_barrier(tuple(jnp.asarray(a, F32) for a in parts))
    return (cos0[None] * cos_k[:, :, None] - sin0[None] * sin_k[:, :, None]).astype(BF16)


def along_tables(devices):
    planes = NX // devices
    waves = np.arange(MX) - MX // 2
    angle = 2 * np.pi * np.mod(np.outer(waves, np.arange(NX)), NX) / NX
    cos = np.cos(angle).reshape(MX, devices, planes)
    sin = np.sin(angle).reshape(MX, devices, planes)
    to_real = np.stack([cos, sin], axis=2)
    to_imag = np.stack([-sin, cos], axis=2)
    forward = np.concatenate([to_real, to_imag], axis=0).reshape(2 * MX, 2 * NX)
    high = forward.astype(jnp.bfloat16).astype(np.float64)
    both = np.concatenate([high, forward - high], axis=0)
    own = jnp.asarray(forward.reshape(2 * MX, devices, 2 * planes).transpose(1, 2, 0), BF16)
    return jnp.asarray(both, BF16), own


def encode_kernel(devices, cap, owner, block, feat, kern, send, slot_of, targets, count):
    pairs = kern.shape[0]
    size = kern.shape[1]

    def clear(d, carry):
        count[d] = 0
        for i in range(cap):
            targets[d * cap + i] = -1
        send[d] = jnp.zeros(send.shape[1:], BF16)
        return carry

    lax.fori_loop(0, devices, clear, 0)

    def one(b, carry):
        values = feat[:, pl.ds(pl.multiple_of(b * size, size), size)]
        for k in range(NBR):
            p = b * NBR + k
            d = owner[p]
            n = count[d]
            count[d] = n + 1
            slot_of[p] = d * cap + n
            targets[d * cap + n] = block[p]
            rows = pl.ds(pl.multiple_of(n * values.shape[0], values.shape[0]), values.shape[0])
            send[d, rows, :] = jnp.dot(values, kern[p], preferred_element_type=F32).astype(BF16)
        return carry

    lax.fori_loop(0, pairs // NBR, one, 0)
    lane = lax.broadcasted_iota(jnp.int32, (NOTE_ROWS, size), 1)

    def note(d, carry):
        row = jnp.zeros((NOTE_ROWS, size), F32)
        for i in range(cap):
            row = jnp.where(lane == i, targets[d * cap + i].astype(F32), row)
        send[d, send.shape[1] - NOTE_ROWS :, :] = row.astype(BF16)
        return carry

    lax.fori_loop(0, devices, note, 0)


def table_tile(table, k, wide):
    return jnp.concatenate([table[k * wide + i] for i in range(wide)], axis=1)


def gather_sums_kernel(cap, channels, per_plane, wide, targets, got, table, field, spec, send, total):
    size = got.shape[2]
    chunk = wide * size
    tiles = table.shape[0] // wide

    def clear(k, carry):
        field[:, pl.ds(pl.multiple_of(k * chunk, chunk), chunk)] = jnp.zeros((field.shape[0], chunk), F32)
        return carry

    lax.fori_loop(0, tiles, clear, 0)

    def add(d, carry):
        for i in range(cap):
            t = targets[d * cap + i]

            @pl.when(t >= 0)
            def _():
                rows = pl.ds(pl.multiple_of(t // per_plane * channels, channels), channels)
                cols = pl.ds(pl.multiple_of(t % per_plane * size, size), size)
                field[rows, cols] += got[d, i * channels : (i + 1) * channels, :].astype(F32)

        return carry

    lax.fori_loop(0, got.shape[0], add, 0)

    def pick(d, carry):
        for i in range(cap):
            t = jnp.maximum(targets[d * cap + i], 0)
            rows = pl.ds(pl.multiple_of(t // per_plane * channels, channels), channels)
            cols = pl.ds(pl.multiple_of(t % per_plane * size, size), size)
            send[d, i] = field[rows, cols].astype(BF16)
        return carry

    lax.fori_loop(0, got.shape[0], pick, 0)
    total[...] = jnp.zeros_like(total)

    def transform(k, carry):
        values = field[:, pl.ds(pl.multiple_of(k * chunk, chunk), chunk)].astype(BF16)
        total[...] += lax.dot_general(table_tile(table, k, wide), values, NT, preferred_element_type=F32)
        return carry

    lax.fori_loop(0, tiles, transform, 0)
    spec[...] = total[...].astype(BF16)


def pen_position(me):
    return me // 4, me // 2 % 2, me % 2


def greet(partners):
    barrier = pltpu.get_barrier_semaphore()
    for d in partners:
        pl.semaphore_signal(barrier, inc=1, device_id={"pen": d}, device_id_type=MESH)
    pl.semaphore_wait(barrier, len(partners))


def quad_partners(me, depth):
    z, y, c = pen_position(me)
    line = [(z + s) % depth * 4 + y * 2 + c for s in range(1, depth)]
    return line, me + 2 - 4 * y, me + 1 - 2 * c


def gather_blocks(me, depth, full, z_send, z_recv, y_send, y_recv, c_send, c_recv, arrived):
    z, y, c = pen_position(me)
    line, side, twin = quad_partners(me, depth)
    started = []

    def push(block, target, send_sem, recv_sem):
        copy = pltpu.make_async_remote_copy(
            src_ref=full.at[block],
            dst_ref=full.at[block],
            send_sem=send_sem,
            recv_sem=recv_sem,
            device_id={"pen": target},
            device_id_type=MESH,
        )
        copy.start()
        started.append(copy)

    def landed(block, send_sem, recv_sem):
        pltpu.make_async_remote_copy(
            src_ref=full.at[block],
            dst_ref=full.at[block],
            send_sem=send_sem,
            recv_sem=recv_sem,
            device_id={"pen": twin},
            device_id_type=MESH,
        ).wait_recv()

    for s in range(1, depth):
        push(me, line[s - 1], z_send.at[s - 1], z_recv.at[s - 1])
    push(me, side, y_send.at[0], y_recv.at[0])
    push(me, twin, c_send.at[0], c_recv.at[0])
    arrived(me)
    for s in range(1, depth):
        block = (z + depth - s) % depth * 4 + y * 2 + c
        landed(block, z_send.at[s - 1], z_recv.at[s - 1])
        push(block, side, y_send.at[s], y_recv.at[s])
        push(block, twin, c_send.at[s], c_recv.at[s])
        arrived(block)
    for s in range(depth):
        block = (z + depth - s) % depth * 4 + (1 - y) * 2 + c
        landed(block, y_send.at[s], y_recv.at[s])
        push(block, twin, c_send.at[depth + s], c_recv.at[depth + s])
        arrived(block)
    for s in range(depth):
        block = (z + depth - s) % depth * 4 + y * 2 + 1 - c
        landed(block, c_send.at[s], c_recv.at[s])
        arrived(block)
    for s in range(depth):
        block = (z + depth - s) % depth * 4 + (1 - y) * 2 + 1 - c
        landed(block, c_send.at[depth + s], c_recv.at[depth + s])
        arrived(block)
    for copy in started:
        copy.wait_send()


def mix_kernel(number, channels, planes, depth, forward, inverse, data, weights, scaling, full, spread_out, weight, fetch_sem, *sems):
    rows = 2 * MX
    here, fan = weight.shape[0], weight.shape[1] // (2 * channels)
    me = lax.axis_index("pen")
    line, side, twin = quad_partners(me, depth)
    fetch = pltpu.make_async_copy(weights.at[pl.ds(number * here, here)], weight, fetch_sem)
    fetch.start()
    greet(line + [side, twin])
    width = 2 * channels
    row_wave = lax.broadcasted_iota(jnp.int32, (rows, width), 0) % MX
    half = lax.broadcasted_iota(jnp.int32, (rows, width), 1) // channels
    left = half == 0
    modes = jnp.dot(forward[...], data[...], preferred_element_type=F32)
    modes = modes[:rows] + modes[rows:]
    fetch.wait()
    for pair in range(here // 2):
        own = modes[:, pair * width : (pair + 1) * width]
        other = pltpu.roll(own, channels, 1)
        halves = []
        for k in range(2):
            twice = jnp.where(left, own, other) if k == 0 else jnp.where(left, other, own)
            spread = jnp.concatenate(
                [jnp.where(row_wave == 2 * f + half, twice, 0.0).astype(BF16) for f in range(fan)], axis=1
            )
            prod = jnp.dot(spread, weight[2 * pair + k], preferred_element_type=F32)
            real, imag = prod[:MX], prod[MX:]
            real_turned = pltpu.roll(real, channels, 1)
            imag_turned = pltpu.roll(imag, channels, 1)
            if k == 0:
                halves.append((real - imag_turned, real_turned + imag))
            else:
                halves.append((real_turned - imag, real + imag_turned))
        (real_a, imag_a), (real_b, imag_b) = halves
        top = left[:MX]
        both = jnp.concatenate([jnp.where(top, real_a, real_b), jnp.where(top, imag_a, imag_b)], axis=0)
        both = (both * scaling[:, pair * width : (pair + 1) * width]).astype(BF16)
        full[me, :, pair * width : (pair + 1) * width] = both

    def arrived(block):
        spread_out[block] = jnp.dot(inverse[0], full[block], preferred_element_type=F32).astype(BF16)

    gather_blocks(me, depth, full, *sems, arrived)


def gelu_twice(v):
    scale = math.sqrt(2.0 / math.pi)
    turn = jnp.tanh(v * (BF16(scale) + BF16(scale * 0.044715) * (v * v)))
    return v + v * turn


def layer_kernel(devices, planes, wide, modes, table, field, up, down, picked, spec, fetched, total, summed, out, own_sem, send_sem, recv_sem):
    channels = field.shape[0] // planes
    me = lax.axis_index("pen")
    step, steps = pl.program_id(0), pl.num_programs(0)

    def exchange(j):
        return pltpu.make_async_remote_copy(
            src_ref=picked.at[(me + j) % devices],
            dst_ref=fetched.at[me],
            send_sem=send_sem.at[j],
            recv_sem=recv_sem.at[j],
            device_id={"pen": (me + j) % devices},
            device_id_type=MESH,
        )

    own = pltpu.make_async_copy(picked.at[me], fetched.at[me], own_sem)

    @pl.when(step == 0)
    def _():
        total[...] = jnp.zeros_like(total)
        greet([(me + j) % devices for j in range(1, devices)])
        own.start()
        for j in range(1, devices):
            exchange(j).start()

    tile = table_tile(table, 0, wide)
    summed[...] = field[...] + jnp.dot(modes[...], tile, preferred_element_type=F32)
    down_half = (down[...].astype(F32) * 0.5).astype(BF16)

    def raise_up(p):
        values = summed[p * channels : (p + 1) * channels, :]
        return jnp.dot(up[...], values.astype(BF16), preferred_element_type=F32).astype(BF16)

    ahead = raise_up(0)
    for p in range(planes):
        v = ahead
        if p + 1 < planes:
            ahead = raise_up(p + 1)
        rows = slice(p * channels, (p + 1) * channels)
        values = summed[rows, :] + jnp.dot(down_half, gelu_twice(v), preferred_element_type=F32)
        out[rows, :] = values.astype(BF16)
    total[...] += lax.dot_general(tile, out[...], NT, preferred_element_type=F32)

    @pl.when(step == steps - 1)
    def _():
        spec[...] = total[...].astype(BF16)
        own.wait()
        for j in range(1, devices):
            exchange(j).wait_send()
        for j in range(1, devices):
            pltpu.make_async_remote_copy(
                src_ref=picked.at[me],
                dst_ref=fetched.at[(me + devices - j) % devices],
                send_sem=send_sem.at[j],
                recv_sem=recv_sem.at[j],
                device_id={"pen": (me + devices - j) % devices},
                device_id_type=MESH,
            ).wait_recv()


def point_phases(owner, block, planes, per_plane, lines_here):
    x = owner * planes + block // per_plane
    y = (block % per_plane)[None, :] * lines_here + jnp.arange(lines_here, dtype=jnp.int32)[:, None]
    wave_x = jnp.arange(MX, dtype=jnp.int32) - MX // 2
    wave_y = jnp.arange(MY, dtype=jnp.int32) - MY // 2
    turns_x = jnp.mod(x[:, None] * wave_x[None, :], NX).astype(F32) / NX
    turns_y = jnp.mod(y[:, :, None] * wave_y[None, None, :], NY).astype(F32) / NY
    angle = 2 * math.pi * (turns_x[None, :, None, :] + turns_y[:, :, :, None])
    cos, sin = jnp.cos(angle), jnp.sin(angle)
    real = jnp.stack([cos, -sin], axis=3)
    imag = jnp.stack([sin, cos], axis=3)
    rows = 2 * lines_here * x.shape[0]
    return jnp.stack([real, imag], axis=0).reshape(rows, MY * 2 * MX).astype(BF16)


def depth_table(size):
    lines_here = size // NZ
    wave = np.arange(MZ)
    cell = np.arange(size)
    angle = 2 * np.pi * np.mod(np.outer(wave, cell % NZ), NZ) / NZ
    on_line = (cell // NZ)[None, :] == np.arange(lines_here)[:, None]
    parts = np.stack([np.cos(angle), -np.sin(angle)], axis=1)
    full = parts[:, :, None, :] * on_line[None, None, :, :]
    full = full.reshape(MZ // 2, 2, 2 * lines_here, size).transpose(0, 2, 1, 3)
    return jnp.asarray(full.reshape(MZ // 2 * 2 * lines_here, 2 * size), BF16)


def answer_kernel(channels, group, slot_of, got, kern, phases, first, second, depths, up, down, out, waves):
    size = kern.shape[1]
    pairs = kern.shape[0]
    tall = phases.shape[0]
    lane = 2 * channels
    per_group = first.shape[2] // lane
    for number, full in enumerate((first, second)):
        for g in range(full.shape[0]):
            for w in range(per_group):
                part = jnp.dot(phases[...], full[g, :, w * lane : (w + 1) * lane], preferred_element_type=F32)
                start = (g * per_group + w) * tall
                waves[number, start : start + tall, :] = part
    count = waves.shape[1] // pairs

    def spectral(number, p):
        value = waves[number, pl.ds(p, count, stride=pairs), :].astype(BF16)
        wide = lax.dot_general(value, depths[...], TN, preferred_element_type=F32)
        return wide[:channels, :size] + wide[channels:, size:]

    downs = [(down[n].astype(F32) * 0.5).astype(BF16) for n in range(LAYERS)]

    def body(b, carry):
        todo = [(b * group + i) * NBR + k for i in range(group) for k in range(NBR)]
        values = jnp.concatenate([got[slot_of[p]].astype(F32) for p in todo], axis=1)
        for n in range(LAYERS):
            summed = values + jnp.concatenate([spectral(n, p) for p in todo], axis=1)
            v = jnp.dot(up[n], summed.astype(BF16), preferred_element_type=F32).astype(BF16)
            values = summed + jnp.dot(downs[n], gelu_twice(v), preferred_element_type=F32)
        values = values.astype(BF16)
        for i in range(group):
            acc = None
            for k in range(NBR):
                at = (i * NBR + k) * size
                term = lax.dot_general(values[:, at : at + size], kern[todo[i * NBR + k]], NT, preferred_element_type=F32)
                acc = term if acc is None else acc + term
            out[:, pl.ds(pl.multiple_of((b * group + i) * size, size), size)] = acc
        return carry

    lax.fori_loop(0, pairs // NBR // group, body, 0)


def swap(values):
    return lax.all_to_all(values, "pen", split_axis=0, concat_axis=0, tiled=True)


def per_device(point_feat, pair_kernel, pair_owner, pair_block, spec_weight, mlp_up, mlp_down):
    devices = lax.axis_size("pen")
    pairs, size = pair_kernel.shape[0], pair_kernel.shape[1]
    channels = point_feat.shape[0]
    cap = 2 * pairs // devices
    planes = NX // devices
    plane_cells = NY * NZ
    per_plane = plane_cells // size
    here = spec_weight.shape[1]
    modes_all = MY * MZ
    hidden = mlp_up.shape[1]
    lines = planes * channels
    wide = 4
    table = plane_table(devices, size)
    forward, inverse = along_tables(devices)

    send, slot_of, targets = pl.pallas_call(
        functools.partial(encode_kernel, devices, cap),
        out_shape=(
            jax.ShapeDtypeStruct((devices, cap * channels + NOTE_ROWS, size), BF16),
            jax.ShapeDtypeStruct((pairs,), jnp.int32),
            jax.ShapeDtypeStruct((devices * cap,), jnp.int32),
        ),
        in_specs=[SMEM, SMEM, VMEM, VMEM],
        out_specs=(VMEM, SMEM, SMEM),
        scratch_shapes=[pltpu.SMEM((devices,), jnp.int32)],
        name="encode",
    )(pair_owner[:, 0], pair_block, point_feat, pair_kernel)
    got = swap(send)
    wanted = got[:, cap * channels, :cap].astype(jnp.int32).reshape(devices * cap)

    field, spec, picked = pl.pallas_call(
        functools.partial(gather_sums_kernel, cap, channels, per_plane, wide),
        out_shape=(
            jax.ShapeDtypeStruct((lines, plane_cells), F32),
            jax.ShapeDtypeStruct((2 * modes_all, lines), BF16),
            jax.ShapeDtypeStruct((devices, cap, channels, size), BF16),
        ),
        in_specs=[SMEM, VMEM, VMEM],
        out_specs=(VMEM, VMEM, VMEM),
        scratch_shapes=[pltpu.VMEM((2 * modes_all, lines), F32)],
        name="place",
    )(wanted, got, table)

    me = lax.axis_index("pen")
    depth = devices // 4
    wave_z = (me * here + jnp.arange(here * channels, dtype=jnp.int32) // channels) % MZ
    scaling = (jnp.where(wave_z == 0, 1.0, 2.0).astype(F32) / (NX * NY * NZ))[None, :]
    weights = spec_weight.reshape(LAYERS * here, MX * channels, 2 * channels)
    own_inverse = lax.dynamic_slice_in_dim(inverse, me, 1, axis=0)
    lines_here = size // NZ
    phases = point_phases(pair_owner[:, 0], pair_block, planes, per_plane, lines_here)
    fulls = []
    for number in range(LAYERS):
        last = number == LAYERS - 1
        across = swap(spec.reshape(devices, 2 * here, lines))
        data = across.reshape(devices, 2, here, planes, channels).transpose(0, 1, 3, 2, 4)
        full, modes = pl.pallas_call(
            functools.partial(mix_kernel, number, channels, planes, depth),
            out_shape=(
                jax.ShapeDtypeStruct((devices, 2 * MX, here * channels), BF16),
                jax.ShapeDtypeStruct((devices, 2 * planes, here * channels), BF16),
            ),
            in_specs=[VMEM, VMEM, VMEM, ANY, VMEM],
            out_specs=(VMEM, VMEM),
            scratch_shapes=[
                pltpu.VMEM((here, MX * channels, 2 * channels), BF16),
                pltpu.SemaphoreType.DMA,
                pltpu.SemaphoreType.DMA((depth - 1,)),
                pltpu.SemaphoreType.DMA((depth - 1,)),
                pltpu.SemaphoreType.DMA((depth,)),
                pltpu.SemaphoreType.DMA((depth,)),
                pltpu.SemaphoreType.DMA((2 * depth,)),
                pltpu.SemaphoreType.DMA((2 * depth,)),
            ],
            compiler_params=pltpu.CompilerParams(collective_id=number, has_side_effects=True),
            name="mix",
        )(forward, own_inverse, data.reshape(2 * NX, here * channels), weights, scaling)
        fulls.append(full.reshape(MY, MZ // here, 2 * MX, here * channels).transpose(1, 0, 2, 3).reshape(MZ // here, MY * 2 * MX, here * channels))
        if last:
            break
        modes = modes.reshape(devices, 2, planes, here, channels).transpose(0, 1, 3, 2, 4)
        modes = modes.reshape(2 * modes_all, lines).T

        chunk = wide * size
        spec_shape = (2 * modes_all, lines)
        spec, fetched = pl.pallas_call(
            functools.partial(layer_kernel, devices, planes, wide),
            out_shape=(
                jax.ShapeDtypeStruct(spec_shape, BF16),
                jax.ShapeDtypeStruct((devices, cap, channels, size), BF16),
            ),
            grid=(plane_cells // chunk,),
            in_specs=[
                pl.BlockSpec((lines, 2 * modes_all), lambda k: (0, 0)),
                pl.BlockSpec((wide, 2 * modes_all, size), lambda k: (k, 0, 0)),
                pl.BlockSpec((lines, chunk), lambda k: (0, k)),
                pl.BlockSpec((hidden, channels), lambda k: (0, 0)),
                pl.BlockSpec((channels, hidden), lambda k: (0, 0)),
                ANY,
            ],
            out_specs=(pl.BlockSpec(spec_shape, lambda k: (0, 0)), ANY),
            scratch_shapes=[
                pltpu.VMEM(spec_shape, F32),
                pltpu.VMEM((lines, chunk), F32),
                pltpu.VMEM((lines, chunk), BF16),
                pltpu.SemaphoreType.DMA,
                pltpu.SemaphoreType.DMA((devices,)),
                pltpu.SemaphoreType.DMA((devices,)),
            ],
            compiler_params=pltpu.CompilerParams(collective_id=LAYERS + number, has_side_effects=True),
            name="layer",
        )(modes, table, field, mlp_up[number], mlp_down[number], picked)

    return pl.pallas_call(
        functools.partial(answer_kernel, channels, 2),
        out_shape=jax.ShapeDtypeStruct((channels, pairs // NBR * size), F32),
        in_specs=[SMEM] + [VMEM] * 8,
        out_specs=VMEM,
        scratch_shapes=[pltpu.VMEM((LAYERS, MZ // 2 * 2 * lines_here * pairs, 2 * channels), F32)],
        name="answer",
    )(slot_of, fetched.reshape(devices * cap, channels, size), pair_kernel, phases, *fulls, depth_table(size), mlp_up, mlp_down)


def solution(mesh):
    in_specs = (
        P(None, ("groups", "pen")),
        P(("groups", "pen"), None, None),
        P(("groups", "pen"), None),
        P(("groups", "pen")),
        P(None, "pen", None, None, None),
        P(),
        P(),
    )
    out_specs = P(None, ("groups", "pen"))
    return jax.shard_map(
        per_device, mesh=mesh, in_specs=in_specs, out_specs=out_specs, check_vma=False
    )
```

```python
import functools
import math

import jax
import jax.numpy as jnp
import numpy as np
from jax import lax
from jax.experimental import pallas as pl
from jax.experimental.pallas import tpu as pltpu
from jax.sharding import PartitionSpec as P

NX = 128
NY = 64
NZ = 64
MX = 16
MY = 16
MZ = 16
LAYERS = 2
NBR = 4
NOTE_ROWS = 16

F32 = jnp.float32
BF16 = jnp.bfloat16
VMEM = pl.BlockSpec(memory_space=pltpu.VMEM)
SMEM = pl.BlockSpec(memory_space=pltpu.SMEM)
NT = (((1,), (1,)), ((), ()))
TN = (((0,), (0,)), ((), ()))
MESH = pl.DeviceIdType.MESH
ANY = pl.BlockSpec(memory_space=pl.ANY)


def plane_table(devices, lanes):
    here = MY * MZ // devices
    row = np.arange(2 * MY * MZ)
    mode = row // (2 * here) * here + row % here
    imag = (row % (2 * here)) // here
    wave_y = mode // MZ - MY // 2
    wave_z = mode % MZ
    cell = np.arange(lanes)
    turns = np.mod(np.outer(wave_y, cell // NZ), NY) / NY + np.mod(np.outer(wave_z, cell % NZ), NZ) / NZ
    first = 2 * np.pi * turns + np.where(imag, np.pi / 2, 0.0)[:, None]
    tiles = NY * NZ // lanes
    step = 2 * np.pi * np.mod(np.outer(np.arange(tiles) * (lanes // NZ), wave_y), NY) / NY
    parts = [np.cos(first), np.sin(first), np.cos(step), np.sin(step)]
    cos0, sin0, cos_k, sin_k = lax.optimization_barrier(tuple(jnp.asarray(a, F32) for a in parts))
    return (cos0[None] * cos_k[:, :, None] - sin0[None] * sin_k[:, :, None]).astype(BF16)


def along_tables(devices):
    planes = NX // devices
    waves = np.arange(MX) - MX // 2
    angle = 2 * np.pi * np.mod(np.outer(waves, np.arange(NX)), NX) / NX
    cos = np.cos(angle).reshape(MX, devices, planes)
    sin = np.sin(angle).reshape(MX, devices, planes)
    to_real = np.stack([cos, sin], axis=2)
    to_imag = np.stack([-sin, cos], axis=2)
    forward = np.concatenate([to_real, to_imag], axis=0).reshape(2 * MX, 2 * NX)
    high = forward.astype(jnp.bfloat16).astype(np.float64)
    both = np.concatenate([high, forward - high], axis=0)
    own = jnp.asarray(forward.reshape(2 * MX, devices, 2 * planes).transpose(1, 2, 0), BF16)
    return jnp.asarray(both, BF16), own


def encode_kernel(devices, cap, owner, block, feat, kern, send, slot_of, targets, count):
    pairs = kern.shape[0]
    size = kern.shape[1]

    def clear(d, carry):
        count[d] = 0
        for i in range(cap):
            targets[d * cap + i] = -1
        send[d] = jnp.zeros(send.shape[1:], BF16)
        return carry

    lax.fori_loop(0, devices, clear, 0)

    def one(b, carry):
        values = feat[:, pl.ds(pl.multiple_of(b * size, size), size)]
        for k in range(NBR):
            p = b * NBR + k
            d = owner[p]
            n = count[d]
            count[d] = n + 1
            slot_of[p] = d * cap + n
            targets[d * cap + n] = block[p]
            rows = pl.ds(pl.multiple_of(n * values.shape[0], values.shape[0]), values.shape[0])
            send[d, rows, :] = jnp.dot(values, kern[p], preferred_element_type=F32).astype(BF16)
        return carry

    lax.fori_loop(0, pairs // NBR, one, 0)
    lane = lax.broadcasted_iota(jnp.int32, (NOTE_ROWS, size), 1)

    def note(d, carry):
        row = jnp.zeros((NOTE_ROWS, size), F32)
        for i in range(cap):
            row = jnp.where(lane == i, targets[d * cap + i].astype(F32), row)
        send[d, send.shape[1] - NOTE_ROWS :, :] = row.astype(BF16)
        return carry

    lax.fori_loop(0, devices, note, 0)


def table_tile(table, k, wide):
    return jnp.concatenate([table[k * wide + i] for i in range(wide)], axis=1)


def gather_sums_kernel(cap, channels, per_plane, wide, targets, got, table, field, spec, send, total):
    size = got.shape[2]
    chunk = wide * size
    tiles = table.shape[0] // wide

    def clear(k, carry):
        field[:, pl.ds(pl.multiple_of(k * chunk, chunk), chunk)] = jnp.zeros((field.shape[0], chunk), F32)
        return carry

    lax.fori_loop(0, tiles, clear, 0)

    def add(d, carry):
        for i in range(cap):
            t = targets[d * cap + i]

            @pl.when(t >= 0)
            def _():
                rows = pl.ds(pl.multiple_of(t // per_plane * channels, channels), channels)
                cols = pl.ds(pl.multiple_of(t % per_plane * size, size), size)
                field[rows, cols] += got[d, i * channels : (i + 1) * channels, :].astype(F32)

        return carry

    lax.fori_loop(0, got.shape[0], add, 0)

    def pick(d, carry):
        for i in range(cap):
            t = jnp.maximum(targets[d * cap + i], 0)
            rows = pl.ds(pl.multiple_of(t // per_plane * channels, channels), channels)
            cols = pl.ds(pl.multiple_of(t % per_plane * size, size), size)
            send[d, i] = field[rows, cols].astype(BF16)
        return carry

    lax.fori_loop(0, got.shape[0], pick, 0)
    total[...] = jnp.zeros_like(total)

    def transform(k, carry):
        values = field[:, pl.ds(pl.multiple_of(k * chunk, chunk), chunk)].astype(BF16)
        total[...] += lax.dot_general(table_tile(table, k, wide), values, NT, preferred_element_type=F32)
        return carry

    lax.fori_loop(0, tiles, transform, 0)
    spec[...] = total[...].astype(BF16)


def pen_position(me):
    return me // 4, me // 2 % 2, me % 2


def greet(partners):
    barrier = pltpu.get_barrier_semaphore()
    for d in partners:
        pl.semaphore_signal(barrier, inc=1, device_id={"pen": d}, device_id_type=MESH)
    pl.semaphore_wait(barrier, len(partners))


def quad_partners(me, depth):
    z, y, c = pen_position(me)
    line = [(z + s) % depth * 4 + y * 2 + c for s in range(1, depth)]
    return line, me + 2 - 4 * y, me + 1 - 2 * c


def gather_blocks(me, depth, full, z_send, z_recv, y_send, y_recv, c_send, c_recv, arrived):
    z, y, c = pen_position(me)
    line, side, twin = quad_partners(me, depth)
    started = []

    def push(block, target, send_sem, recv_sem):
        copy = pltpu.make_async_remote_copy(
            src_ref=full.at[block],
            dst_ref=full.at[block],
            send_sem=send_sem,
            recv_sem=recv_sem,
            device_id={"pen": target},
            device_id_type=MESH,
        )
        copy.start()
        started.append(copy)

    def landed(block, send_sem, recv_sem):
        pltpu.make_async_remote_copy(
            src_ref=full.at[block],
            dst_ref=full.at[block],
            send_sem=send_sem,
            recv_sem=recv_sem,
            device_id={"pen": twin},
            device_id_type=MESH,
        ).wait_recv()

    for s in range(1, depth):
        push(me, line[s - 1], z_send.at[s - 1], z_recv.at[s - 1])
    push(me, side, y_send.at[0], y_recv.at[0])
    push(me, twin, c_send.at[0], c_recv.at[0])
    arrived(me)
    for s in range(1, depth):
        block = (z + depth - s) % depth * 4 + y * 2 + c
        landed(block, z_send.at[s - 1], z_recv.at[s - 1])
        push(block, side, y_send.at[s], y_recv.at[s])
        push(block, twin, c_send.at[s], c_recv.at[s])
        arrived(block)
    for s in range(depth):
        block = (z + depth - s) % depth * 4 + (1 - y) * 2 + c
        landed(block, y_send.at[s], y_recv.at[s])
        push(block, twin, c_send.at[depth + s], c_recv.at[depth + s])
        arrived(block)
    for s in range(depth):
        block = (z + depth - s) % depth * 4 + y * 2 + 1 - c
        landed(block, c_send.at[s], c_recv.at[s])
        arrived(block)
    for s in range(depth):
        block = (z + depth - s) % depth * 4 + (1 - y) * 2 + 1 - c
        landed(block, c_send.at[depth + s], c_recv.at[depth + s])
        arrived(block)
    for copy in started:
        copy.wait_send()


def mix_modes(channels, spread_of, weight, scaling, full, me):
    rows = 2 * MX
    width = 2 * channels
    left = lax.broadcasted_iota(jnp.int32, (rows, width), 1) < channels
    for pair in range(weight.shape[0] // 2):
        halves = []
        for k in range(2):
            prod = jnp.dot(spread_of(2 * pair + k), weight[2 * pair + k], preferred_element_type=F32)
            real, imag = prod[:MX], prod[MX:]
            real_turned = pltpu.roll(real, channels, 1)
            imag_turned = pltpu.roll(imag, channels, 1)
            if k == 0:
                halves.append((real - imag_turned, real_turned + imag))
            else:
                halves.append((real_turned - imag, real + imag_turned))
        (real_a, imag_a), (real_b, imag_b) = halves
        top = left[:MX]
        both = jnp.concatenate([jnp.where(top, real_a, real_b), jnp.where(top, imag_a, imag_b)], axis=0)
        both = (both * scaling[:, pair * width : (pair + 1) * width]).astype(BF16)
        full[me, :, pair * width : (pair + 1) * width] = both


def mix_kernel(number, channels, planes, depth, forward, inverse, data, weights, scaling, full, spread_out, weight, fetch_sem, *sems):
    rows = 2 * MX
    here, fan = weight.shape[0], weight.shape[1] // (2 * channels)
    me = lax.axis_index("pen")
    line, side, twin = quad_partners(me, depth)
    fetch = pltpu.make_async_copy(weights.at[pl.ds(number * here, here)], weight, fetch_sem)
    fetch.start()
    greet(line + [side, twin])
    width = 2 * channels
    row_wave = lax.broadcasted_iota(jnp.int32, (rows, width), 0) % MX
    half = lax.broadcasted_iota(jnp.int32, (rows, width), 1) // channels
    left = half == 0
    modes = jnp.dot(forward[...], data[...], preferred_element_type=F32)
    modes = modes[:rows] + modes[rows:]
    fetch.wait()

    def spread_of(m):
        own = modes[:, m // 2 * width : (m // 2 + 1) * width]
        other = pltpu.roll(own, channels, 1)
        twice = jnp.where(left, own, other) if m % 2 == 0 else jnp.where(left, other, own)
        return jnp.concatenate(
            [jnp.where(row_wave == 2 * f + half, twice, 0.0).astype(BF16) for f in range(fan)], axis=1
        )

    mix_modes(channels, spread_of, weight, scaling, full, me)

    def arrived(block):
        spread_out[block] = jnp.dot(inverse[0], full[block], preferred_element_type=F32).astype(BF16)

    gather_blocks(me, depth, full, *sems, arrived)


def gelu_twice(v):
    scale = math.sqrt(2.0 / math.pi)
    turn = jnp.tanh(v * (BF16(scale) + BF16(scale * 0.044715) * (v * v)))
    return v + v * turn


def local_table(planes, channels):
    waves = np.arange(MX) - MX // 2
    angle = 2 * np.pi * np.mod(np.outer(np.arange(planes), waves), NX) / NX
    cos, sin = jnp.asarray(np.cos(angle), F32), jnp.asarray(np.sin(angle), F32)
    parts = lax.optimization_barrier((cos, sin))
    quarter = MX // 4
    both = jnp.stack([a.reshape(planes, 4, quarter) for a in parts], axis=2)
    same = (jnp.arange(channels)[:, None] == jnp.arange(channels)[None, :])[None, :, None, None, None, :]
    wide = jnp.where(same, both[:, None, :, :, :, None], 0.0)
    return wide.reshape(planes * channels, 4, 2 * quarter * channels).transpose(1, 0, 2).astype(BF16)


def turn_table(devices, channels):
    waves = np.arange(MX) - MX // 2
    angle = 2 * np.pi * np.mod(np.outer(np.arange(devices) * (NX // devices), waves), NX) / NX
    parts = np.stack([np.cos(angle), np.sin(angle)], axis=1)
    return jnp.repeat(jnp.asarray(parts, F32), channels, axis=2)


def along_modes(across, local, turns, here):
    devices, lines = across.shape[0], across.shape[2]
    values = across[...].reshape(devices * 2 * here, lines)
    reals, imags = [], []
    for q in range(local.shape[0]):
        prod = jnp.dot(values, local[q], preferred_element_type=F32)
        width = prod.shape[1] // 2
        real, imag = None, None
        for d in range(devices):
            base = d * 2 * here
            rc, rs = prod[base : base + here, :width], prod[base : base + here, width:]
            ic, is_ = prod[base + here : base + 2 * here, :width], prod[base + here : base + 2 * here, width:]
            own_real, own_imag = rc + is_, ic - rs
            cos = turns[d, 0:1, q * width : (q + 1) * width]
            sin = turns[d, 1:2, q * width : (q + 1) * width]
            add_real = own_real * cos + own_imag * sin
            add_imag = own_imag * cos - own_real * sin
            real = add_real if real is None else real + add_real
            imag = add_imag if imag is None else imag + add_imag
        reals.append(real)
        imags.append(imag)
    return jnp.concatenate(reals, axis=1), jnp.concatenate(imags, axis=1)


def offsets(devices):
    return [(dz, dy, dc) for dz in range(devices // 4) for dy in range(2) for dc in range(2) if dz + dy + dc]


def shifted(me, devices, offset, sign):
    z, y, c = pen_position(me)
    dz, dy, dc = offset
    depth = devices // 4
    return (z + (dz if sign > 0 else depth - dz)) % depth * 4 + (y + dy) % 2 * 2 + (c + dc) % 2


def layer_kernel(
    number, devices, planes, wide,
    modes, table, field, up, down, local, turns, scaling, picked, weights,
    fetched, full_out,
    total, summed, out, spec, across, weight, full,
    own_sem, fetch_sem, send_sem, recv_sem, spec_send, spec_recv, *sems,
):
    channels = field.shape[0] // planes
    here = weight.shape[0]
    me = lax.axis_index("pen")
    step, steps = pl.program_id(0), pl.num_programs(0)
    order = offsets(devices)
    depth = devices // 4

    def exchange(j):
        peer = shifted(me, devices, order[j], 1)
        return pltpu.make_async_remote_copy(
            src_ref=picked.at[peer],
            dst_ref=fetched.at[me],
            send_sem=send_sem.at[j],
            recv_sem=recv_sem.at[j],
            device_id={"pen": peer},
            device_id_type=MESH,
        )

    def arrival(j):
        peer = shifted(me, devices, order[j], -1)
        return pltpu.make_async_remote_copy(
            src_ref=picked.at[peer],
            dst_ref=fetched.at[peer],
            send_sem=send_sem.at[j],
            recv_sem=recv_sem.at[j],
            device_id={"pen": peer},
            device_id_type=MESH,
        )

    def spec_exchange(j):
        peer = shifted(me, devices, order[j], 1)
        return pltpu.make_async_remote_copy(
            src_ref=spec.at[peer],
            dst_ref=across.at[me],
            send_sem=spec_send.at[j],
            recv_sem=spec_recv.at[j],
            device_id={"pen": peer},
            device_id_type=MESH,
        )

    def spec_arrival(j):
        peer = shifted(me, devices, order[j], -1)
        return pltpu.make_async_remote_copy(
            src_ref=spec.at[peer],
            dst_ref=across.at[peer],
            send_sem=spec_send.at[j],
            recv_sem=spec_recv.at[j],
            device_id={"pen": peer},
            device_id_type=MESH,
        )

    def when_early(o):
        dz, dy, dc = o
        if 2 * dz < depth:
            return 0
        return 1 if 2 * dz > depth and dc == 0 else 2

    early = [j for j, o in enumerate(order) if when_early(o) == 0 or when_early(o) == 1]
    middle = [j for j, o in enumerate(order) if j not in early and 2 * o[0] > depth]
    late = [j for j, o in enumerate(order) if j not in early and j not in middle]
    own = pltpu.make_async_copy(picked.at[me], fetched.at[me], own_sem)
    fetch = pltpu.make_async_copy(weights.at[pl.ds(number * here, here)], weight, fetch_sem)

    @pl.when(step == 0)
    def _():
        total[...] = jnp.zeros_like(total)
        greet([shifted(me, devices, o, 1) for o in order])
        own.start()
        fetch.start()
        for j in early:
            exchange(j).start()

    tile = table_tile(table, 0, wide)
    summed[...] = field[...] + jnp.dot(modes[...], tile, preferred_element_type=F32)
    down_half = (down[...].astype(F32) * 0.5).astype(BF16)

    def raise_up(p):
        values = summed[p * channels : (p + 1) * channels, :]
        return jnp.dot(up[...], values.astype(BF16), preferred_element_type=F32).astype(BF16)

    ahead = raise_up(0)
    for p in range(planes):
        v = ahead
        if p + 1 < planes:
            ahead = raise_up(p + 1)
        rows = slice(p * channels, (p + 1) * channels)
        values = summed[rows, :] + jnp.dot(down_half, gelu_twice(v), preferred_element_type=F32)
        out[rows, :] = values.astype(BF16)
    total[...] += lax.dot_general(tile, out[...], NT, preferred_element_type=F32)

    @pl.when(step == steps - 1)
    def _():
        for d in range(devices):
            spec[d] = total[d * 2 * here : (d + 1) * 2 * here, :].astype(BF16)
        across[me] = spec[me]
        for j in range(len(order)):
            spec_exchange(j).start()
        for j in middle:
            exchange(j).start()
        own.wait()
        fetch.wait()
        for j in range(len(order)):
            spec_arrival(j).wait_recv()
        real, imag = along_modes(across, local, turns, here)
        lanes = MX * channels
        keep = lax.broadcasted_iota(jnp.int32, (MX, lanes), 0) == lax.broadcasted_iota(jnp.int32, (MX, lanes), 1) // channels

        def spread_of(m):
            top = jnp.where(keep, real[m : m + 1, :], 0.0).astype(BF16)
            low = jnp.where(keep, imag[m : m + 1, :], 0.0).astype(BF16)
            return jnp.concatenate([top, low], axis=0)

        mix_modes(channels, spread_of, weight, scaling, full, me)

        def arrived(block):
            if block is me:
                for j in late:
                    exchange(j).start()

        gather_blocks(me, depth, full, *sems, arrived)
        back = pltpu.make_async_copy(full, full_out, own_sem)
        back.start()
        for j in range(len(order)):
            spec_exchange(j).wait_send()
        for j in range(len(order)):
            exchange(j).wait_send()
        for j in range(len(order)):
            arrival(j).wait_recv()
        back.wait()


def point_phases(owner, block, planes, per_plane, lines_here):
    x = owner * planes + block // per_plane
    y = (block % per_plane)[None, :] * lines_here + jnp.arange(lines_here, dtype=jnp.int32)[:, None]
    wave_x = jnp.arange(MX, dtype=jnp.int32) - MX // 2
    wave_y = jnp.arange(MY, dtype=jnp.int32) - MY // 2
    turns_x = jnp.mod(x[:, None] * wave_x[None, :], NX).astype(F32) / NX
    turns_y = jnp.mod(y[:, :, None] * wave_y[None, None, :], NY).astype(F32) / NY
    angle = 2 * math.pi * (turns_x[None, :, None, :] + turns_y[:, :, :, None])
    cos, sin = jnp.cos(angle), jnp.sin(angle)
    real = jnp.stack([cos, -sin], axis=3)
    imag = jnp.stack([sin, cos], axis=3)
    rows = 2 * lines_here * x.shape[0]
    return jnp.stack([real, imag], axis=0).reshape(rows, MY * 2 * MX).astype(BF16)


def depth_table(size):
    lines_here = size // NZ
    wave = np.arange(MZ)
    cell = np.arange(size)
    angle = 2 * np.pi * np.mod(np.outer(wave, cell % NZ), NZ) / NZ
    on_line = (cell // NZ)[None, :] == np.arange(lines_here)[:, None]
    parts = np.stack([np.cos(angle), -np.sin(angle)], axis=1)
    full = parts[:, :, None, :] * on_line[None, None, :, :]
    full = full.reshape(MZ // 2, 2, 2 * lines_here, size).transpose(0, 2, 1, 3)
    return jnp.asarray(full.reshape(MZ // 2 * 2 * lines_here, 2 * size), BF16)


def answer_kernel(channels, group, slot_of, got, kern, phases, first, second, depths, up, down, out, waves):
    size = kern.shape[1]
    pairs = kern.shape[0]
    tall = phases.shape[0]
    lane = 2 * channels
    per_group = first.shape[2] // lane
    for number, full in enumerate((first, second)):
        for g in range(full.shape[0]):
            for w in range(per_group):
                part = jnp.dot(phases[...], full[g, :, w * lane : (w + 1) * lane], preferred_element_type=F32)
                start = (g * per_group + w) * tall
                waves[number, start : start + tall, :] = part
    count = waves.shape[1] // pairs

    def spectral(number, p):
        value = waves[number, pl.ds(p, count, stride=pairs), :].astype(BF16)
        wide = lax.dot_general(value, depths[...], TN, preferred_element_type=F32)
        return wide[:channels, :size] + wide[channels:, size:]

    downs = [(down[n].astype(F32) * 0.5).astype(BF16) for n in range(LAYERS)]

    def body(b, carry):
        todo = [(b * group + i) * NBR + k for i in range(group) for k in range(NBR)]
        values = jnp.concatenate([got[slot_of[p]].astype(F32) for p in todo], axis=1)
        for n in range(LAYERS):
            summed = values + jnp.concatenate([spectral(n, p) for p in todo], axis=1)
            v = jnp.dot(up[n], summed.astype(BF16), preferred_element_type=F32).astype(BF16)
            values = summed + jnp.dot(downs[n], gelu_twice(v), preferred_element_type=F32)
        values = values.astype(BF16)
        for i in range(group):
            acc = None
            for k in range(NBR):
                at = (i * NBR + k) * size
                term = lax.dot_general(values[:, at : at + size], kern[todo[i * NBR + k]], NT, preferred_element_type=F32)
                acc = term if acc is None else acc + term
            out[:, pl.ds(pl.multiple_of((b * group + i) * size, size), size)] = acc
        return carry

    lax.fori_loop(0, pairs // NBR // group, body, 0)


def swap(values):
    return lax.all_to_all(values, "pen", split_axis=0, concat_axis=0, tiled=True)


def per_device(point_feat, pair_kernel, pair_owner, pair_block, spec_weight, mlp_up, mlp_down):
    devices = lax.axis_size("pen")
    pairs, size = pair_kernel.shape[0], pair_kernel.shape[1]
    channels = point_feat.shape[0]
    cap = 2 * pairs // devices
    planes = NX // devices
    plane_cells = NY * NZ
    per_plane = plane_cells // size
    here = spec_weight.shape[1]
    modes_all = MY * MZ
    hidden = mlp_up.shape[1]
    lines = planes * channels
    wide = 4
    table = plane_table(devices, size)
    forward, inverse = along_tables(devices)

    send, slot_of, targets = pl.pallas_call(
        functools.partial(encode_kernel, devices, cap),
        out_shape=(
            jax.ShapeDtypeStruct((devices, cap * channels + NOTE_ROWS, size), BF16),
            jax.ShapeDtypeStruct((pairs,), jnp.int32),
            jax.ShapeDtypeStruct((devices * cap,), jnp.int32),
        ),
        in_specs=[SMEM, SMEM, VMEM, VMEM],
        out_specs=(VMEM, SMEM, SMEM),
        scratch_shapes=[pltpu.SMEM((devices,), jnp.int32)],
        name="encode",
    )(pair_owner[:, 0], pair_block, point_feat, pair_kernel)
    got = swap(send)
    wanted = got[:, cap * channels, :cap].astype(jnp.int32).reshape(devices * cap)

    field, spec, picked = pl.pallas_call(
        functools.partial(gather_sums_kernel, cap, channels, per_plane, wide),
        out_shape=(
            jax.ShapeDtypeStruct((lines, plane_cells), F32),
            jax.ShapeDtypeStruct((2 * modes_all, lines), BF16),
            jax.ShapeDtypeStruct((devices, cap, channels, size), BF16),
        ),
        in_specs=[SMEM, VMEM, VMEM],
        out_specs=(VMEM, VMEM, VMEM),
        scratch_shapes=[pltpu.VMEM((2 * modes_all, lines), F32)],
        name="place",
    )(wanted, got, table)

    me = lax.axis_index("pen")
    depth = devices // 4
    wave_z = (me * here + jnp.arange(here * channels, dtype=jnp.int32) // channels) % MZ
    scaling = (jnp.where(wave_z == 0, 1.0, 2.0).astype(F32) / (NX * NY * NZ))[None, :]
    weights = spec_weight.reshape(LAYERS * here, MX * channels, 2 * channels)
    own_inverse = lax.dynamic_slice_in_dim(inverse, me, 1, axis=0)
    lines_here = size // NZ
    phases = point_phases(pair_owner[:, 0], pair_block, planes, per_plane, lines_here)
    gather_sems = [
        pltpu.SemaphoreType.DMA((depth - 1,)),
        pltpu.SemaphoreType.DMA((depth - 1,)),
        pltpu.SemaphoreType.DMA((depth,)),
        pltpu.SemaphoreType.DMA((depth,)),
        pltpu.SemaphoreType.DMA((2 * depth,)),
        pltpu.SemaphoreType.DMA((2 * depth,)),
    ]
    full_shape = (devices, 2 * MX, here * channels)
    weight_shape = (here, MX * channels, 2 * channels)
    across = swap(spec.reshape(devices, 2 * here, lines))
    data = across.reshape(devices, 2, here, planes, channels).transpose(0, 1, 3, 2, 4)
    first, modes = pl.pallas_call(
        functools.partial(mix_kernel, 0, channels, planes, depth),
        out_shape=(
            jax.ShapeDtypeStruct(full_shape, BF16),
            jax.ShapeDtypeStruct((devices, 2 * planes, here * channels), BF16),
        ),
        in_specs=[VMEM, VMEM, VMEM, ANY, VMEM],
        out_specs=(VMEM, VMEM),
        scratch_shapes=[pltpu.VMEM(weight_shape, BF16), pltpu.SemaphoreType.DMA] + gather_sems,
        compiler_params=pltpu.CompilerParams(collective_id=0, has_side_effects=True),
        name="mix",
    )(forward, own_inverse, data.reshape(2 * NX, here * channels), weights, scaling)
    modes = modes.reshape(devices, 2, planes, here, channels).transpose(0, 1, 3, 2, 4)
    modes = modes.reshape(2 * modes_all, lines).T

    chunk = wide * size
    local = local_table(planes, channels)
    turns = turn_table(devices, channels)
    whole = lambda shape: pl.BlockSpec(shape, lambda k: (0,) * len(shape))
    peers = devices - 1
    fetched, second = pl.pallas_call(
        functools.partial(layer_kernel, 1, devices, planes, wide),
        out_shape=(
            jax.ShapeDtypeStruct((devices, cap, channels, size), BF16),
            jax.ShapeDtypeStruct(full_shape, BF16),
        ),
        grid=(plane_cells // chunk,),
        in_specs=[
            whole((lines, 2 * modes_all)),
            pl.BlockSpec((wide, 2 * modes_all, size), lambda k: (k, 0, 0)),
            pl.BlockSpec((lines, chunk), lambda k: (0, k)),
            whole((hidden, channels)),
            whole((channels, hidden)),
            whole(local.shape),
            whole(turns.shape),
            whole(scaling.shape),
            ANY,
            ANY,
        ],
        out_specs=(ANY, ANY),
        scratch_shapes=[
            pltpu.VMEM((2 * modes_all, lines), F32),
            pltpu.VMEM((lines, chunk), F32),
            pltpu.VMEM((lines, chunk), BF16),
            pltpu.VMEM((devices, 2 * here, lines), BF16),
            pltpu.VMEM((devices, 2 * here, lines), BF16),
            pltpu.VMEM(weight_shape, BF16),
            pltpu.VMEM(full_shape, BF16),
            pltpu.SemaphoreType.DMA,
            pltpu.SemaphoreType.DMA,
            pltpu.SemaphoreType.DMA((peers,)),
            pltpu.SemaphoreType.DMA((peers,)),
            pltpu.SemaphoreType.DMA((peers,)),
            pltpu.SemaphoreType.DMA((peers,)),
        ]
        + gather_sems,
        compiler_params=pltpu.CompilerParams(collective_id=1, has_side_effects=True),
        name="layer",
    )(modes, table, field, mlp_up[0], mlp_down[0], local, turns, scaling, picked, weights)

    groups_z = MZ // here
    by_wave = lambda full: full.reshape(MY, groups_z, 2 * MX, here * channels).transpose(1, 0, 2, 3).reshape(groups_z, MY * 2 * MX, here * channels)
    fulls = [by_wave(first), by_wave(second)]
    return pl.pallas_call(
        functools.partial(answer_kernel, channels, 2),
        out_shape=jax.ShapeDtypeStruct((channels, pairs // NBR * size), F32),
        in_specs=[SMEM] + [VMEM] * 8,
        out_specs=VMEM,
        scratch_shapes=[pltpu.VMEM((LAYERS, MZ // 2 * 2 * lines_here * pairs, 2 * channels), F32)],
        name="answer",
    )(slot_of, fetched.reshape(devices * cap, channels, size), pair_kernel, phases, *fulls, depth_table(size), mlp_up, mlp_down)


def solution(mesh):
    in_specs = (
        P(None, ("groups", "pen")),
        P(("groups", "pen"), None, None),
        P(("groups", "pen"), None),
        P(("groups", "pen")),
        P(None, "pen", None, None, None),
        P(),
        P(),
    )
    out_specs = P(None, ("groups", "pen"))
    return jax.shard_map(
        per_device, mesh=mesh, in_specs=in_specs, out_specs=out_specs, check_vma=False
    )
```

```python
import functools
import math

import jax
import jax.numpy as jnp
import numpy as np
from jax import lax
from jax.experimental import pallas as pl
from jax.experimental.pallas import tpu as pltpu
from jax.sharding import PartitionSpec as P

NX = 128
NY = 64
NZ = 64
MX = 16
MY = 16
MZ = 16
LAYERS = 2
NBR = 4

F32 = jnp.float32
BF16 = jnp.bfloat16
VMEM = pl.BlockSpec(memory_space=pltpu.VMEM)
SMEM = pl.BlockSpec(memory_space=pltpu.SMEM)
NT = (((1,), (1,)), ((), ()))
TN = (((0,), (0,)), ((), ()))
MESH = pl.DeviceIdType.MESH
ANY = pl.BlockSpec(memory_space=pl.ANY)


def lists_kernel(devices, cap, planes, per_plane, lines_here, owner, block, owners, blocks, order, source, slot_of, notes, xy, targets, count):
    pairs = owner.shape[0]

    def clear(d, carry):
        count[d] = 0
        for i in range(cap):
            targets[d * cap + i] = -1
            order[d * cap + i] = 0
            source[d * cap + i] = 0
        return carry

    lax.fori_loop(0, devices, clear, 0)

    def one(p, carry):
        d = owner[p]
        n = count[d]
        count[d] = n + 1
        slot_of[p] = d * cap + n
        order[d * cap + n] = p
        source[d * cap + n] = lax.div(p, NBR)
        targets[d * cap + n] = block[p]
        return carry

    lax.fori_loop(0, pairs, one, 0)
    lane = lax.broadcasted_iota(jnp.int32, notes.shape[1:], 1)

    def note(d, carry):
        row = jnp.zeros(notes.shape[1:], jnp.int32)
        for i in range(cap):
            row = jnp.where(lane == i, targets[d * cap + i], row)
        notes[d] = row
        return carry

    lax.fori_loop(0, devices, note, 0)
    x = owners[...] * planes + lax.div(blocks[...], per_plane)
    y = lax.rem(blocks[...], per_plane) * lines_here
    xy[0:1, :] = jnp.concatenate([x] * lines_here, axis=1)
    xy[1:2, :] = jnp.concatenate([y + i for i in range(lines_here)], axis=1)


def turn(count, wave, place, span):
    return lax.rem((wave + span - count // 2) * place, span).astype(F32) * (2 * math.pi / span)


def point_phases(xy, phases):
    lanes = xy.shape[1]
    wave = lax.broadcasted_iota(jnp.int32, (MX, lanes), 0)
    angle_x = turn(MX, wave, xy[0:1, :], NX)
    cos_x, sin_x = jnp.cos(angle_x), jnp.sin(angle_x)
    for ky in range(MY):
        angle_y = turn(MY, jnp.full((1, lanes), ky, jnp.int32), xy[1:2, :], NY)
        cos_y, sin_y = jnp.cos(angle_y), jnp.sin(angle_y)
        cos = cos_x * cos_y - sin_x * sin_y
        sin = sin_x * cos_y + cos_x * sin_y
        top = jnp.concatenate([cos, sin], axis=1)
        low = jnp.concatenate([-sin, cos], axis=1)
        phases[ky * 2 * MX : (ky + 1) * 2 * MX, :] = jnp.concatenate([top, low], axis=0).astype(BF16)


def fill_table(here, table, cos_now, sin_now, cos_step, sin_step):
    shape = cos_now.shape
    row = lax.broadcasted_iota(jnp.int32, shape, 0)
    cell = lax.broadcasted_iota(jnp.int32, shape, 1)
    mode = lax.div(row, 2 * here) * here + lax.rem(row, here)
    imag = lax.div(lax.rem(row, 2 * here), here).astype(F32) * (math.pi / 2)
    wave_y, wave_z = lax.div(mode, MZ), lax.rem(mode, MZ)
    angle = turn(MY, wave_y, lax.div(cell, NZ), NY) + turn(0, wave_z, lax.rem(cell, NZ), NZ) + imag
    cos_now[...], sin_now[...] = jnp.cos(angle), jnp.sin(angle)
    step = turn(MY, wave_y, jnp.full(shape, shape[1] // NZ, jnp.int32), NY)
    cos_step[...], sin_step[...] = jnp.cos(step), jnp.sin(step)

    def one(k, carry):
        cos, sin = cos_now[...], sin_now[...]
        table[k] = cos.astype(BF16)
        cos_now[...] = cos * cos_step[...] - sin * sin_step[...]
        sin_now[...] = sin * cos_step[...] + cos * sin_step[...]
        return carry

    lax.fori_loop(0, table.shape[0], one, 0)


def lay_lines(channels, planes, here, spread, lines_now, out):
    width = 2 * channels
    lines = planes * channels
    left = lax.broadcasted_iota(jnp.int32, (planes, width), 1) < channels
    keep = lax.broadcasted_iota(jnp.int32, (planes, lines), 0) == lax.broadcasted_iota(jnp.int32, (planes, lines), 1) // channels
    picks = lax.broadcasted_iota(jnp.int32, (here, here * planes), 0) == lax.broadcasted_iota(jnp.int32, (here, here * planes), 1) // planes
    picks = jnp.where(picks, 1.0, 0.0).astype(BF16)

    def one(d, carry):
        for half in range(2):
            values = spread[d, half * planes : (half + 1) * planes, :]
            pieces = []
            for m in range(here):
                own = values[:, m // 2 * width : (m // 2 + 1) * width]
                other = pltpu.roll(own, channels, 1)
                twice = jnp.where(left, own, other) if m % 2 == 0 else jnp.where(left, other, own)
                pieces.append(jnp.where(keep, jnp.concatenate([twice] * (planes // 2), axis=1), 0.0))
            stack = jnp.concatenate(pieces, axis=0).astype(BF16)
            start = pl.multiple_of(d * 2 * here + half * here, here)
            lines_now[pl.ds(start, here), :] = jnp.dot(picks, stack, preferred_element_type=F32)
        return carry

    lax.fori_loop(0, spread.shape[0], one, 0)
    out[...] = lines_now[...].T.astype(BF16)


def encode_kernel(
    devices, cap, planes,
    order, source, notes, xy, feat, kern, depths, inverse, weights,
    got, notes_in, full_out, lines_out, phases, table_out,
    feats, send, waves, part, part_send, from_twin, kept, side_send, from_side, line_send, from_line,
    weight, full, spread, lines_now, table, cos_now, sin_now, cos_step, sin_step,
    own_sem, fetch_sem, full_sem, table_sem, send_sem, recv_sem, note_send, note_recv,
    twin_send_sem, twin_recv_sem, side_send_sem, side_recv_sem, line_send_sem, line_recv_sem, *sems,
):
    pairs, size = kern.shape[0], kern.shape[1]
    channels = feat.shape[0]
    here = weight.shape[0]
    depth = devices // 4
    me = lax.axis_index("pen")
    z, y, c = pen_position(me)
    line, side, twin = quad_partners(me, depth)
    away = offsets(devices)

    def copy_to(peer, src, dst, send_one, recv_one):
        return pltpu.make_async_remote_copy(
            src_ref=src, dst_ref=dst, send_sem=send_one, recv_sem=recv_one, device_id={"pen": peer}, device_id_type=MESH
        )

    def fill(peer):
        for i in range(cap):
            block = jnp.dot(feats[source[peer * cap + i]], kern[order[peer * cap + i]], preferred_element_type=F32)
            send[peer, i * channels : (i + 1) * channels, :] = block.astype(BF16)

    def exchange(j):
        peer = shifted(me, devices, away[j], 1)
        return copy_to(peer, send.at[peer], got.at[me], send_sem.at[j], recv_sem.at[j])

    def arrival(j):
        peer = shifted(me, devices, away[j], -1)
        return copy_to(peer, send.at[peer], got.at[peer], send_sem.at[j], recv_sem.at[j])

    def note_exchange(j):
        peer = shifted(me, devices, away[j], 1)
        return copy_to(peer, notes.at[peer], notes_in.at[me], note_send.at[j], note_recv.at[j])

    def note_arrival(j):
        peer = shifted(me, devices, away[j], -1)
        return copy_to(peer, notes.at[peer], notes_in.at[peer], note_send.at[j], note_recv.at[j])

    far = [j for j, o in enumerate(away) if 2 * o[0] == depth]
    soon = [j for j in far if away[j][2] == 0]
    later = [j for j in far if away[j][2] == 1]
    rest = [j for j in range(len(away)) if j not in far]

    greet([shifted(me, devices, o, 1) for o in away])
    fetch = pltpu.make_async_copy(weights.at[pl.ds(0, here)], weight, fetch_sem)
    fetch.start()
    for b in range(pairs // NBR):
        feats[b] = feat[:, b * size : (b + 1) * size]
    for j in soon:
        fill(shifted(me, devices, away[j], 1))
    for j in soon:
        exchange(j).start()

    point_phases(xy, phases)
    count = waves.shape[0] // pairs

    def transform(b, carry):
        values = feats[b]
        for k in range(NBR):
            p = b * NBR + k
            block = jnp.dot(values, kern[p], preferred_element_type=F32).astype(BF16)
            both = lax.dot_general(depths[...], block, NT, preferred_element_type=F32)
            waves[pl.ds(p, count, stride=pairs), :] = jnp.concatenate([both[:count], both[count:]], axis=1)
        return carry

    lax.fori_loop(0, pairs // NBR, transform, 0)
    tall = phases.shape[1]
    lane = 2 * channels
    groups_z, per_group = MZ // here, here // 2
    for w in range(MZ // 2):
        values = waves[w * tall : (w + 1) * tall, :].astype(BF16)
        sums = jnp.dot(phases[...], values, preferred_element_type=F32)
        cols = slice(w % per_group * lane, (w % per_group + 1) * lane)
        for ky in range(MY):
            d = ky * groups_z + w // per_group
            block = sums[ky * 2 * MX : (ky + 1) * 2 * MX, :]
            part[d, :, cols] = block
            part_send[d, :, cols] = block.astype(BF16)

    def at(z2, y2, c2):
        return z2 * 4 + y2 * 2 + c2

    walk = list(range(1, depth)) + [0]
    sent = []
    twins, sides, lines = {}, {}, {}
    for s in walk:
        z2 = (z + s) % depth
        for f in range(2):
            y2 = (y + 1 + f) % 2
            twins[s, f] = copy_to(
                twin, part_send.at[at(z2, y2, 1 - c)], from_twin.at[z2 * 2 + y2], twin_send_sem.at[2 * s + f], twin_recv_sem.at[2 * s + f]
            )
            twins[s, f].start()
    for j in later:
        fill(shifted(me, devices, away[j], 1))
    for s in walk:
        z2 = (z + s) % depth
        twins[s, 0].wait_recv()
        side_send[z2] = (part[at(z2, 1 - y, c)] + from_twin[z2 * 2 + 1 - y].astype(F32)).astype(BF16)
        twins[s, 1].wait_recv()
        kept[z2] = part[at(z2, y, c)] + from_twin[z2 * 2 + y].astype(F32)
        sides[s] = copy_to(side, side_send.at[z2], from_side.at[z2], side_send_sem.at[s], side_recv_sem.at[s])
        sides[s].start()
    for s in walk:
        z2 = (z + s) % depth
        sides[s].wait_recv()
        if s:
            line_send[z2] = (kept[z2] + from_side[z2].astype(F32)).astype(BF16)
            lines[s] = copy_to(at(z2, y, c), line_send.at[z2], from_line.at[z], line_send_sem.at[s - 1], line_recv_sem.at[s - 1])
            lines[s].start()
    for j in later:
        exchange(j).start()
    for j in rest:
        fill(shifted(me, devices, away[j], 1))
    fill(me)
    own = pltpu.make_async_copy(send.at[me], got.at[me], own_sem)
    own.start()
    notes_in[me] = notes[me]
    modes = kept[z] + from_side[z].astype(F32)
    for s in range(1, depth):
        z2 = (z + depth - s) % depth
        copy_to(at(z2, y, c), line_send.at[z2], from_line.at[z2], line_send_sem.at[s - 1], line_recv_sem.at[s - 1]).wait_recv()
        modes = modes + from_line[z2].astype(F32)
    fetch.wait()

    rows = 2 * MX
    row_wave = lax.broadcasted_iota(jnp.int32, (rows, lane), 0) % MX
    half = lax.broadcasted_iota(jnp.int32, (rows, lane), 1) // channels
    left = half == 0
    fan = MX // 2

    def spread_of(m):
        mine = modes[:, m // 2 * lane : (m // 2 + 1) * lane]
        other = pltpu.roll(mine, channels, 1)
        twice = jnp.where(left, mine, other) if m % 2 == 0 else jnp.where(left, other, mine)
        return jnp.concatenate(
            [jnp.where(row_wave == 2 * f + half, twice, 0.0).astype(BF16) for f in range(fan)], axis=1
        )

    mix_modes(channels, spread_of, weight, mode_scale(me, here, channels), full, me)

    def arrived(block):
        if block is me:
            for j in rest:
                exchange(j).start()
            for j in range(len(away)):
                note_exchange(j).start()
        spread[block] = jnp.dot(inverse[me], full[block], preferred_element_type=F32)

    gather_blocks(me, depth, full, *sems, arrived)
    back = pltpu.make_async_copy(full, full_out, full_sem)
    back.start()
    lay_lines(channels, planes, here, spread, lines_now, lines_out)
    fill_table(here, table, cos_now, sin_now, cos_step, sin_step)
    put = pltpu.make_async_copy(table, table_out, table_sem)
    put.start()
    for s in walk:
        for f in range(2):
            twins[s, f].wait_send()
        sides[s].wait_send()
        if s:
            lines[s].wait_send()
    for j in range(len(away)):
        note_exchange(j).wait_send()
        note_arrival(j).wait_recv()
        exchange(j).wait_send()
        arrival(j).wait_recv()
    own.wait()
    back.wait()
    put.wait()


def table_tile(table, k, wide):
    return jnp.concatenate([table[k * wide + i] for i in range(wide)], axis=1)


def place_kernel(cap, channels, per_plane, targets, got, field, send):
    size = got.shape[2]

    def clear(k, carry):
        field[:, pl.ds(pl.multiple_of(k * size, size), size)] = jnp.zeros((field.shape[0], size), F32)
        return carry

    lax.fori_loop(0, field.shape[1] // size, clear, 0)

    def add(d, carry):
        for i in range(cap):
            t = targets[d, 0, i]

            @pl.when(t >= 0)
            def _():
                rows = pl.ds(pl.multiple_of(t // per_plane * channels, channels), channels)
                cols = pl.ds(pl.multiple_of(t % per_plane * size, size), size)
                field[rows, cols] += got[d, i * channels : (i + 1) * channels, :].astype(F32)

        return carry

    lax.fori_loop(0, got.shape[0], add, 0)

    def pick(d, carry):
        for i in range(cap):
            t = jnp.maximum(targets[d, 0, i], 0)
            rows = pl.ds(pl.multiple_of(t // per_plane * channels, channels), channels)
            cols = pl.ds(pl.multiple_of(t % per_plane * size, size), size)
            send[d, i] = field[rows, cols].astype(BF16)
        return carry

    lax.fori_loop(0, got.shape[0], pick, 0)


def pen_position(me):
    return me // 4, me // 2 % 2, me % 2


def greet(partners):
    barrier = pltpu.get_barrier_semaphore()
    for d in partners:
        pl.semaphore_signal(barrier, inc=1, device_id={"pen": d}, device_id_type=MESH)
    pl.semaphore_wait(barrier, len(partners))


def quad_partners(me, depth):
    z, y, c = pen_position(me)
    line = [(z + s) % depth * 4 + y * 2 + c for s in range(1, depth)]
    return line, me + 2 - 4 * y, me + 1 - 2 * c


def gather_blocks(me, depth, full, z_send, z_recv, y_send, y_recv, c_send, c_recv, arrived):
    z, y, c = pen_position(me)
    line, side, twin = quad_partners(me, depth)
    started = []

    def push(block, target, send_sem, recv_sem):
        copy = pltpu.make_async_remote_copy(
            src_ref=full.at[block],
            dst_ref=full.at[block],
            send_sem=send_sem,
            recv_sem=recv_sem,
            device_id={"pen": target},
            device_id_type=MESH,
        )
        copy.start()
        started.append(copy)

    def landed(block, send_sem, recv_sem):
        pltpu.make_async_remote_copy(
            src_ref=full.at[block],
            dst_ref=full.at[block],
            send_sem=send_sem,
            recv_sem=recv_sem,
            device_id={"pen": twin},
            device_id_type=MESH,
        ).wait_recv()

    for s in range(1, depth):
        push(me, line[s - 1], z_send.at[s - 1], z_recv.at[s - 1])
    push(me, side, y_send.at[0], y_recv.at[0])
    push(me, twin, c_send.at[0], c_recv.at[0])
    arrived(me)
    for s in range(1, depth):
        block = (z + depth - s) % depth * 4 + y * 2 + c
        landed(block, z_send.at[s - 1], z_recv.at[s - 1])
        push(block, side, y_send.at[s], y_recv.at[s])
        push(block, twin, c_send.at[s], c_recv.at[s])
        arrived(block)
    for s in range(depth):
        block = (z + depth - s) % depth * 4 + (1 - y) * 2 + c
        landed(block, y_send.at[s], y_recv.at[s])
        push(block, twin, c_send.at[depth + s], c_recv.at[depth + s])
        arrived(block)
    for s in range(depth):
        block = (z + depth - s) % depth * 4 + y * 2 + 1 - c
        landed(block, c_send.at[s], c_recv.at[s])
        arrived(block)
    for s in range(depth):
        block = (z + depth - s) % depth * 4 + (1 - y) * 2 + 1 - c
        landed(block, c_send.at[depth + s], c_recv.at[depth + s])
        arrived(block)
    for copy in started:
        copy.wait_send()


def mix_modes(channels, spread_of, weight, scaling, full, me):
    rows = 2 * MX
    width = 2 * channels
    left = lax.broadcasted_iota(jnp.int32, (rows, width), 1) < channels
    for pair in range(weight.shape[0] // 2):
        halves = []
        for k in range(2):
            prod = jnp.dot(spread_of(2 * pair + k), weight[2 * pair + k], preferred_element_type=F32)
            real, imag = prod[:MX], prod[MX:]
            real_turned = pltpu.roll(real, channels, 1)
            imag_turned = pltpu.roll(imag, channels, 1)
            if k == 0:
                halves.append((real - imag_turned, real_turned + imag))
            else:
                halves.append((real_turned - imag, real + imag_turned))
        (real_a, imag_a), (real_b, imag_b) = halves
        top = left[:MX]
        both = jnp.concatenate([jnp.where(top, real_a, real_b), jnp.where(top, imag_a, imag_b)], axis=0)
        both = (both * scaling[:, pair * width : (pair + 1) * width]).astype(BF16)
        full[me, :, pair * width : (pair + 1) * width] = both


def mode_scale(me, here, channels):
    cell = lax.broadcasted_iota(jnp.int32, (1, here * channels), 1)
    wave_z = lax.rem(me * here + lax.div(cell, channels), MZ)
    return jnp.where(wave_z == 0, 1.0, 2.0) * (1.0 / (NX * NY * NZ))


def gelu_twice(v):
    scale = math.sqrt(2.0 / math.pi)
    turn = jnp.tanh(v * (BF16(scale) + BF16(scale * 0.044715) * (v * v)))
    return v + v * turn


def local_rows(planes, channels):
    waves = np.arange(MX) - MX // 2
    angle = 2 * np.pi * np.mod(np.outer(np.arange(planes), waves), NX) / NX
    quarter = MX // 4
    both = np.stack([np.cos(angle).reshape(planes, 4, quarter), np.sin(angle).reshape(planes, 4, quarter)], axis=2)
    return jnp.asarray(np.repeat(both.reshape(planes, 4, 2 * quarter), channels, axis=2).transpose(1, 0, 2), F32)


def fill_local(channels, rows, local):
    lanes = rows.shape[2]
    same = lax.broadcasted_iota(jnp.int32, (channels, lanes), 0) == lax.broadcasted_iota(jnp.int32, (channels, lanes), 1) % channels
    for q in range(rows.shape[0]):
        for p in range(rows.shape[1]):
            local[q, p * channels : (p + 1) * channels, :] = jnp.where(same, rows[q, p : p + 1, :], 0.0).astype(BF16)


def turn_table(devices, channels):
    waves = np.arange(MX) - MX // 2
    angle = 2 * np.pi * np.mod(np.outer(np.arange(devices) * (NX // devices), waves), NX) / NX
    parts = np.stack([np.cos(angle), np.sin(angle)], axis=1)
    return jnp.repeat(jnp.asarray(parts, F32), channels, axis=2)


def along_modes(across, local, turns, here):
    devices, lines = across.shape[0], across.shape[2]
    values = across[...].reshape(devices * 2 * here, lines)
    reals, imags = [], []
    for q in range(local.shape[0]):
        prod = jnp.dot(values, local[q], preferred_element_type=F32)
        width = prod.shape[1] // 2
        real, imag = None, None
        for d in range(devices):
            base = d * 2 * here
            rc, rs = prod[base : base + here, :width], prod[base : base + here, width:]
            ic, is_ = prod[base + here : base + 2 * here, :width], prod[base + here : base + 2 * here, width:]
            own_real, own_imag = rc + is_, ic - rs
            cos = turns[d, 0:1, q * width : (q + 1) * width]
            sin = turns[d, 1:2, q * width : (q + 1) * width]
            add_real = own_real * cos + own_imag * sin
            add_imag = own_imag * cos - own_real * sin
            real = add_real if real is None else real + add_real
            imag = add_imag if imag is None else imag + add_imag
        reals.append(real)
        imags.append(imag)
    return jnp.concatenate(reals, axis=1), jnp.concatenate(imags, axis=1)


def offsets(devices):
    return [(dz, dy, dc) for dz in range(devices // 4) for dy in range(2) for dc in range(2) if dz + dy + dc]


def shifted(me, devices, offset, sign):
    z, y, c = pen_position(me)
    dz, dy, dc = offset
    depth = devices // 4
    return (z + (dz if sign > 0 else depth - dz)) % depth * 4 + (y + dy) % 2 * 2 + (c + dc) % 2


def layer_kernel(
    number, devices, planes, wide,
    modes, table, field, up, down, local_small, turns, picked, weights,
    fetched, full_out,
    total, summed, out, spec, across, weight, full, local,
    own_sem, fetch_sem, send_sem, recv_sem, spec_send, spec_recv, *sems,
):
    channels = field.shape[0] // planes
    here = weight.shape[0]
    me = lax.axis_index("pen")
    step, steps = pl.program_id(0), pl.num_programs(0)
    order = offsets(devices)
    depth = devices // 4

    def exchange(j):
        peer = shifted(me, devices, order[j], 1)
        return pltpu.make_async_remote_copy(
            src_ref=picked.at[peer],
            dst_ref=fetched.at[me],
            send_sem=send_sem.at[j],
            recv_sem=recv_sem.at[j],
            device_id={"pen": peer},
            device_id_type=MESH,
        )

    def arrival(j):
        peer = shifted(me, devices, order[j], -1)
        return pltpu.make_async_remote_copy(
            src_ref=picked.at[peer],
            dst_ref=fetched.at[peer],
            send_sem=send_sem.at[j],
            recv_sem=recv_sem.at[j],
            device_id={"pen": peer},
            device_id_type=MESH,
        )

    def spec_exchange(j):
        peer = shifted(me, devices, order[j], 1)
        return pltpu.make_async_remote_copy(
            src_ref=spec.at[peer],
            dst_ref=across.at[me],
            send_sem=spec_send.at[j],
            recv_sem=spec_recv.at[j],
            device_id={"pen": peer},
            device_id_type=MESH,
        )

    def spec_arrival(j):
        peer = shifted(me, devices, order[j], -1)
        return pltpu.make_async_remote_copy(
            src_ref=spec.at[peer],
            dst_ref=across.at[peer],
            send_sem=spec_send.at[j],
            recv_sem=spec_recv.at[j],
            device_id={"pen": peer},
            device_id_type=MESH,
        )

    def when_early(o):
        dz, dy, dc = o
        if 2 * dz < depth:
            return 0
        return 1 if 2 * dz > depth and dc == 0 else 2

    early = [j for j, o in enumerate(order) if when_early(o) == 0 or when_early(o) == 1]
    middle = [j for j, o in enumerate(order) if j not in early and 2 * o[0] > depth]
    late = [j for j, o in enumerate(order) if j not in early and j not in middle]
    own = pltpu.make_async_copy(picked.at[me], fetched.at[me], own_sem)
    fetch = pltpu.make_async_copy(weights.at[pl.ds(number * here, here)], weight, fetch_sem)

    @pl.when(step == 0)
    def _():
        total[...] = jnp.zeros_like(total)
        greet([shifted(me, devices, o, 1) for o in order])
        own.start()
        fetch.start()
        for j in early:
            exchange(j).start()
        fill_local(channels, local_small, local)

    tile = table_tile(table, 0, wide)
    summed[...] = field[...] + jnp.dot(modes[...], tile, preferred_element_type=F32)
    down_half = (down[...].astype(F32) * 0.5).astype(BF16)

    def raise_up(p):
        values = summed[p * channels : (p + 1) * channels, :]
        return jnp.dot(up[...], values.astype(BF16), preferred_element_type=F32).astype(BF16)

    ahead = raise_up(0)
    for p in range(planes):
        v = ahead
        if p + 1 < planes:
            ahead = raise_up(p + 1)
        rows = slice(p * channels, (p + 1) * channels)
        values = summed[rows, :] + jnp.dot(down_half, gelu_twice(v), preferred_element_type=F32)
        out[rows, :] = values.astype(BF16)
    total[...] += lax.dot_general(tile, out[...], NT, preferred_element_type=F32)

    @pl.when(step == steps - 1)
    def _():
        for d in range(devices):
            spec[d] = total[d * 2 * here : (d + 1) * 2 * here, :].astype(BF16)
        across[me] = spec[me]
        for j in range(len(order)):
            spec_exchange(j).start()
        for j in middle:
            exchange(j).start()
        own.wait()
        fetch.wait()
        for j in range(len(order)):
            spec_arrival(j).wait_recv()
        real, imag = along_modes(across, local, turns, here)
        lanes = MX * channels
        keep = lax.broadcasted_iota(jnp.int32, (MX, lanes), 0) == lax.broadcasted_iota(jnp.int32, (MX, lanes), 1) // channels

        def spread_of(m):
            top = jnp.where(keep, real[m : m + 1, :], 0.0).astype(BF16)
            low = jnp.where(keep, imag[m : m + 1, :], 0.0).astype(BF16)
            return jnp.concatenate([top, low], axis=0)

        mix_modes(channels, spread_of, weight, mode_scale(me, here, channels), full, me)

        def arrived(block):
            if block is me:
                for j in late:
                    exchange(j).start()

        gather_blocks(me, depth, full, *sems, arrived)
        back = pltpu.make_async_copy(full, full_out, own_sem)
        back.start()
        for j in range(len(order)):
            spec_exchange(j).wait_send()
        for j in range(len(order)):
            exchange(j).wait_send()
        for j in range(len(order)):
            arrival(j).wait_recv()
        back.wait()


def depth_table(size):
    lines_here = size // NZ
    wave = np.arange(MZ)
    cell = np.arange(size)
    angle = 2 * np.pi * np.mod(np.outer(wave, cell % NZ), NZ) / NZ
    on_line = (cell // NZ)[None, :] == np.arange(lines_here)[:, None]
    parts = np.stack([np.cos(angle), -np.sin(angle)], axis=1)
    full = parts[:, :, None, :] * on_line[None, None, :, :]
    full = full.reshape(MZ // 2, 2, 2 * lines_here, size).transpose(0, 2, 1, 3)
    return jnp.asarray(full.reshape(MZ // 2 * 2 * lines_here, 2 * size), BF16)


def answer_kernel(channels, group, slot_of, got, kern, phases, first, second, depths, up, down, out, waves):
    size = kern.shape[1]
    pairs = kern.shape[0]
    turned = phases[...].T
    tall = turned.shape[0]
    lane = 2 * channels
    per_group = first.shape[2] // lane
    for number, full in enumerate((first, second)):
        for g in range(full.shape[0]):
            for w in range(per_group):
                part = jnp.dot(turned, full[g, :, w * lane : (w + 1) * lane], preferred_element_type=F32)
                start = (g * per_group + w) * tall
                waves[number, start : start + tall, :] = part
    count = waves.shape[1] // pairs

    def spectral(number, p):
        value = waves[number, pl.ds(p, count, stride=pairs), :].astype(BF16)
        wide = lax.dot_general(value, depths[...], TN, preferred_element_type=F32)
        return wide[:channels, :size] + wide[channels:, size:]

    downs = [(down[n].astype(F32) * 0.5).astype(BF16) for n in range(LAYERS)]

    def body(b, carry):
        todo = [(b * group + i) * NBR + k for i in range(group) for k in range(NBR)]
        values = jnp.concatenate([got[slot_of[p]].astype(F32) for p in todo], axis=1)
        for n in range(LAYERS):
            summed = values + jnp.concatenate([spectral(n, p) for p in todo], axis=1)
            v = jnp.dot(up[n], summed.astype(BF16), preferred_element_type=F32).astype(BF16)
            values = summed + jnp.dot(downs[n], gelu_twice(v), preferred_element_type=F32)
        values = values.astype(BF16)
        for i in range(group):
            acc = None
            for k in range(NBR):
                at = (i * NBR + k) * size
                term = lax.dot_general(values[:, at : at + size], kern[todo[i * NBR + k]], NT, preferred_element_type=F32)
                acc = term if acc is None else acc + term
            out[:, pl.ds(pl.multiple_of((b * group + i) * size, size), size)] = acc
        return carry

    lax.fori_loop(0, pairs // NBR // group, body, 0)


def plane_inverse(devices):
    planes = NX // devices
    waves = np.arange(MX) - MX // 2
    angle = 2 * np.pi * np.mod(np.outer(np.arange(NX), waves), NX) / NX
    cos, sin = np.cos(angle).reshape(devices, planes, MX), np.sin(angle).reshape(devices, planes, MX)
    real = np.concatenate([cos, -sin], axis=2)
    imag = np.concatenate([sin, cos], axis=2)
    return jnp.asarray(np.concatenate([real, imag], axis=1), BF16)


def per_device(point_feat, pair_kernel, pair_owner, pair_block, spec_weight, mlp_up, mlp_down):
    devices = lax.axis_size("pen")
    pairs, size = pair_kernel.shape[0], pair_kernel.shape[1]
    channels = point_feat.shape[0]
    cap = 2 * pairs // devices
    planes = NX // devices
    plane_cells = NY * NZ
    per_plane = plane_cells // size
    here = spec_weight.shape[1]
    modes_all = MY * MZ
    hidden = mlp_up.shape[1]
    lines = planes * channels
    wide = 4
    lines_here = size // NZ
    depth = devices // 4
    peers = devices - 1
    waves_tall = 2 * lines_here * pairs
    DMA = pltpu.SemaphoreType.DMA
    shape = jax.ShapeDtypeStruct
    weights = spec_weight.reshape(LAYERS * here, MX * channels, 2 * channels)
    depths = depth_table(size)
    depth_rows = depths.shape[0]
    forward_depths = depths.reshape(depth_rows, 2, size).transpose(1, 0, 2).reshape(2 * depth_rows, size)
    owner = pair_owner[:, 0]

    order, source, slot_of, notes, xy = pl.pallas_call(
        functools.partial(lists_kernel, devices, cap, planes, per_plane, lines_here),
        out_shape=(
            shape((devices * cap,), jnp.int32),
            shape((devices * cap,), jnp.int32),
            shape((pairs,), jnp.int32),
            shape((devices, 8, 128), jnp.int32),
            shape((2, lines_here * pairs), jnp.int32),
        ),
        in_specs=[SMEM, SMEM, VMEM, VMEM],
        out_specs=(SMEM, SMEM, SMEM, VMEM, VMEM),
        scratch_shapes=[pltpu.SMEM((devices * cap,), jnp.int32), pltpu.SMEM((devices,), jnp.int32)],
        name="lists",
    )(owner, pair_block, owner.reshape(1, pairs), pair_block.reshape(1, pairs))

    gather_sems = [DMA((depth - 1,)), DMA((depth - 1,)), DMA((depth,)), DMA((depth,)), DMA((2 * depth,)), DMA((2 * depth,))]
    full_shape = (devices, 2 * MX, here * channels)
    weight_shape = (here, MX * channels, 2 * channels)
    table_shape = (plane_cells // size, 2 * modes_all, size)
    block_shape = full_shape[1:]
    trig = pltpu.VMEM((2 * modes_all, size), F32)
    got, wanted, first, modes, phases, table = pl.pallas_call(
        functools.partial(encode_kernel, devices, cap, planes),
        out_shape=(
            shape((devices, cap * channels, size), BF16),
            shape((devices, 8, 128), jnp.int32),
            shape(full_shape, BF16),
            shape((lines, 2 * modes_all), BF16),
            shape((MY * 2 * MX, waves_tall), BF16),
            shape(table_shape, BF16),
        ),
        in_specs=[SMEM] * 2 + [VMEM] * 6 + [ANY],
        out_specs=(ANY, VMEM, ANY, VMEM, VMEM, ANY),
        scratch_shapes=[
            pltpu.VMEM((pairs // NBR, channels, size), BF16),
            pltpu.VMEM((devices, cap * channels, size), BF16),
            pltpu.VMEM((MZ // 2 * waves_tall, 2 * channels), F32),
            pltpu.VMEM(full_shape, F32),
            pltpu.VMEM(full_shape, BF16),
            pltpu.VMEM((2 * depth,) + block_shape, BF16),
            pltpu.VMEM((depth,) + block_shape, F32),
            pltpu.VMEM((depth,) + block_shape, BF16),
            pltpu.VMEM((depth,) + block_shape, BF16),
            pltpu.VMEM((depth,) + block_shape, BF16),
            pltpu.VMEM((depth,) + block_shape, BF16),
            pltpu.VMEM(weight_shape, BF16),
            pltpu.VMEM(full_shape, BF16),
            pltpu.VMEM((devices, 2 * planes, here * channels), F32),
            pltpu.VMEM((2 * modes_all, lines), F32),
            pltpu.VMEM(table_shape, BF16),
            trig,
            trig,
            trig,
            trig,
            DMA,
            DMA,
            DMA,
            DMA,
            DMA((peers,)),
            DMA((peers,)),
            DMA((peers,)),
            DMA((peers,)),
            DMA((2 * depth,)),
            DMA((2 * depth,)),
            DMA((depth,)),
            DMA((depth,)),
            DMA((depth - 1,)),
            DMA((depth - 1,)),
        ]
        + gather_sems,
        compiler_params=pltpu.CompilerParams(collective_id=0, has_side_effects=True),
        name="encode",
    )(order, source, notes, xy, point_feat, pair_kernel, forward_depths, plane_inverse(devices), weights)

    field, picked = pl.pallas_call(
        functools.partial(place_kernel, cap, channels, per_plane),
        out_shape=(shape((lines, plane_cells), F32), shape((devices, cap, channels, size), BF16)),
        in_specs=[SMEM, VMEM],
        out_specs=(VMEM, VMEM),
        name="place",
    )(wanted, got)

    chunk = wide * size
    local_small = local_rows(planes, channels)
    turns = turn_table(devices, channels)
    whole = lambda extent: pl.BlockSpec(extent, lambda k: (0,) * len(extent))
    fetched, second = pl.pallas_call(
        functools.partial(layer_kernel, 1, devices, planes, wide),
        out_shape=(shape((devices, cap, channels, size), BF16), shape(full_shape, BF16)),
        grid=(plane_cells // chunk,),
        in_specs=[
            whole((lines, 2 * modes_all)),
            pl.BlockSpec((wide, 2 * modes_all, size), lambda k: (k, 0, 0)),
            pl.BlockSpec((lines, chunk), lambda k: (0, k)),
            whole((hidden, channels)),
            whole((channels, hidden)),
            whole(local_small.shape),
            whole(turns.shape),
            ANY,
            ANY,
        ],
        out_specs=(ANY, ANY),
        scratch_shapes=[
            pltpu.VMEM((2 * modes_all, lines), F32),
            pltpu.VMEM((lines, chunk), F32),
            pltpu.VMEM((lines, chunk), BF16),
            pltpu.VMEM((devices, 2 * here, lines), BF16),
            pltpu.VMEM((devices, 2 * here, lines), BF16),
            pltpu.VMEM(weight_shape, BF16),
            pltpu.VMEM(full_shape, BF16),
            pltpu.VMEM((local_small.shape[0], lines, local_small.shape[2]), BF16),
            DMA,
            DMA,
            DMA((peers,)),
            DMA((peers,)),
            DMA((peers,)),
            DMA((peers,)),
        ]
        + gather_sems,
        compiler_params=pltpu.CompilerParams(collective_id=1, has_side_effects=True),
        name="layer",
    )(modes, table, field, mlp_up[0], mlp_down[0], local_small, turns, picked, weights)

    groups_z = MZ // here
    by_wave = lambda full: full.reshape(MY, groups_z, 2 * MX, here * channels).transpose(1, 0, 2, 3).reshape(groups_z, MY * 2 * MX, here * channels)
    return pl.pallas_call(
        functools.partial(answer_kernel, channels, 2),
        out_shape=shape((channels, pairs // NBR * size), F32),
        in_specs=[SMEM] + [VMEM] * 8,
        out_specs=VMEM,
        scratch_shapes=[pltpu.VMEM((LAYERS, MZ // 2 * waves_tall, 2 * channels), F32)],
        name="answer",
    )(slot_of, fetched.reshape(devices * cap, channels, size), pair_kernel, phases, by_wave(first), by_wave(second), depths, mlp_up, mlp_down)


def solution(mesh):
    in_specs = (
        P(None, ("groups", "pen")),
        P(("groups", "pen"), None, None),
        P(("groups", "pen"), None),
        P(("groups", "pen")),
        P(None, "pen", None, None, None),
        P(),
        P(),
    )
    out_specs = P(None, ("groups", "pen"))
    return jax.shard_map(
        per_device, mesh=mesh, in_specs=in_specs, out_specs=out_specs, check_vma=False
    )
```

```python
import functools
import math

import jax
import jax.numpy as jnp
import numpy as np
from jax import lax
from jax.experimental import pallas as pl
from jax.experimental.pallas import tpu as pltpu
from jax.sharding import PartitionSpec as P

NX = 128
NY = 64
NZ = 64
MX = 16
MY = 16
MZ = 16
LAYERS = 2
NBR = 4

F32 = jnp.float32
BF16 = jnp.bfloat16
VMEM = pl.BlockSpec(memory_space=pltpu.VMEM)
SMEM = pl.BlockSpec(memory_space=pltpu.SMEM)
NT = (((1,), (1,)), ((), ()))
TN = (((0,), (0,)), ((), ()))
MESH = pl.DeviceIdType.MESH
ANY = pl.BlockSpec(memory_space=pl.ANY)


def lists_kernel(devices, cap, planes, per_plane, lines_here, owner, block, owners, blocks, order, source, slot_of, notes, xy, slots_xy, targets, count):
    pairs = owner.shape[0]

    def clear(d, carry):
        count[d] = 0
        for i in range(cap):
            targets[d * cap + i] = -1
            order[d * cap + i] = 0
            source[d * cap + i] = 0
        return carry

    lax.fori_loop(0, devices, clear, 0)

    def one(p, carry):
        d = owner[p]
        n = count[d]
        count[d] = n + 1
        slot_of[p] = d * cap + n
        order[d * cap + n] = p
        source[d * cap + n] = lax.div(p, NBR)
        targets[d * cap + n] = block[p]
        return carry

    lax.fori_loop(0, pairs, one, 0)
    lane = lax.broadcasted_iota(jnp.int32, notes.shape[1:], 1)

    def note(d, carry):
        row = jnp.zeros(notes.shape[1:], jnp.int32)
        for i in range(cap):
            row = jnp.where(lane == i, targets[d * cap + i], row)
        notes[d] = row
        return carry

    lax.fori_loop(0, devices, note, 0)
    x = owners[...] * planes + lax.div(blocks[...], per_plane)
    y = lax.rem(blocks[...], per_plane) * lines_here
    xy[0:1, :] = jnp.concatenate([x] * lines_here, axis=1)
    xy[1:2, :] = jnp.concatenate([y + i for i in range(lines_here)], axis=1)
    places = lax.broadcasted_iota(jnp.int32, (1, devices * cap), 1)
    row = jnp.zeros((1, devices * cap), jnp.int32)
    for i in range(devices * cap):
        row = jnp.where(places == i, jnp.maximum(targets[i], 0), row)
    x = lax.div(places, cap) * planes + lax.div(row, per_plane)
    y = lax.rem(row, per_plane) * lines_here
    slots_xy[0:1, :] = jnp.concatenate([x] * lines_here, axis=1)
    slots_xy[1:2, :] = jnp.concatenate([y + i for i in range(lines_here)], axis=1)


def turn(count, wave, place, span):
    return lax.rem((wave + span - count // 2) * place, span).astype(F32) * (2 * math.pi / span)


def point_phases(xy, phases):
    lanes = xy.shape[1]
    wave = lax.broadcasted_iota(jnp.int32, (MX, lanes), 0)
    angle_x = turn(MX, wave, xy[0:1, :], NX)
    cos_x, sin_x = jnp.cos(angle_x), jnp.sin(angle_x)
    for ky in range(MY):
        angle_y = turn(MY, jnp.full((1, lanes), ky, jnp.int32), xy[1:2, :], NY)
        cos_y, sin_y = jnp.cos(angle_y), jnp.sin(angle_y)
        cos = cos_x * cos_y - sin_x * sin_y
        sin = sin_x * cos_y + cos_x * sin_y
        top = jnp.concatenate([cos, sin], axis=1)
        low = jnp.concatenate([-sin, cos], axis=1)
        phases[ky * 2 * MX : (ky + 1) * 2 * MX, :] = jnp.concatenate([top, low], axis=0).astype(BF16)


def fill_table(here, table, cos_now, sin_now, cos_step, sin_step):
    shape = cos_now.shape
    row = lax.broadcasted_iota(jnp.int32, shape, 0)
    cell = lax.broadcasted_iota(jnp.int32, shape, 1)
    mode = lax.div(row, 2 * here) * here + lax.rem(row, here)
    imag = lax.div(lax.rem(row, 2 * here), here).astype(F32) * (math.pi / 2)
    wave_y, wave_z = lax.div(mode, MZ), lax.rem(mode, MZ)
    angle = turn(MY, wave_y, lax.div(cell, NZ), NY) + turn(0, wave_z, lax.rem(cell, NZ), NZ) + imag
    cos_now[...], sin_now[...] = jnp.cos(angle), jnp.sin(angle)
    step = turn(MY, wave_y, jnp.full(shape, shape[1] // NZ, jnp.int32), NY)
    cos_step[...], sin_step[...] = jnp.cos(step), jnp.sin(step)

    def one(k, carry):
        cos, sin = cos_now[...], sin_now[...]
        table[k] = cos.astype(BF16)
        cos_now[...] = cos * cos_step[...] - sin * sin_step[...]
        sin_now[...] = sin * cos_step[...] + cos * sin_step[...]
        return carry

    lax.fori_loop(0, table.shape[0], one, 0)


def lay_lines(channels, planes, here, spread, lines_now, out):
    width = 2 * channels
    lines = planes * channels
    left = lax.broadcasted_iota(jnp.int32, (planes, width), 1) < channels
    keep = lax.broadcasted_iota(jnp.int32, (planes, lines), 0) == lax.broadcasted_iota(jnp.int32, (planes, lines), 1) // channels
    picks = lax.broadcasted_iota(jnp.int32, (here, here * planes), 0) == lax.broadcasted_iota(jnp.int32, (here, here * planes), 1) // planes
    picks = jnp.where(picks, 1.0, 0.0).astype(BF16)

    def one(d, carry):
        for half in range(2):
            values = spread[d, half * planes : (half + 1) * planes, :]
            pieces = []
            for m in range(here):
                own = values[:, m // 2 * width : (m // 2 + 1) * width]
                other = pltpu.roll(own, channels, 1)
                twice = jnp.where(left, own, other) if m % 2 == 0 else jnp.where(left, other, own)
                pieces.append(jnp.where(keep, jnp.concatenate([twice] * (planes // 2), axis=1), 0.0))
            stack = jnp.concatenate(pieces, axis=0).astype(BF16)
            start = pl.multiple_of(d * 2 * here + half * here, here)
            lines_now[pl.ds(start, here), :] = jnp.dot(picks, stack, preferred_element_type=F32)
        return carry

    lax.fori_loop(0, spread.shape[0], one, 0)
    out[...] = lines_now[...].T.astype(BF16)


def encode_kernel(
    devices, cap, planes,
    order, source, notes, xy, feat, kern, depths, inverse, weights,
    got, notes_in, full_out, lines_out, table_out,
    phases, feats, send, waves, part, part_send, from_twin, kept, side_send, from_side, line_send, from_line,
    weight, full, spread, lines_now, table, cos_now, sin_now, cos_step, sin_step,
    own_sem, fetch_sem, full_sem, table_sem, send_sem, recv_sem, note_send, note_recv, *sems,
):
    pairs, size = kern.shape[0], kern.shape[1]
    channels = feat.shape[0]
    here = weight.shape[0]
    depth = devices // 4
    me = lax.axis_index("pen")
    away = offsets(devices)

    def fill(peer):
        for i in range(cap):
            block = jnp.dot(feats[source[peer * cap + i]], kern[order[peer * cap + i]], preferred_element_type=F32)
            send[peer, i * channels : (i + 1) * channels, :] = block.astype(BF16)

    def exchange(j):
        peer = shifted(me, devices, away[j], 1)
        return copy_to(peer, send.at[peer], got.at[me], send_sem.at[j], recv_sem.at[j])

    def arrival(j):
        peer = shifted(me, devices, away[j], -1)
        return copy_to(peer, send.at[peer], got.at[peer], send_sem.at[j], recv_sem.at[j])

    def note_exchange(j):
        peer = shifted(me, devices, away[j], 1)
        return copy_to(peer, notes.at[peer], notes_in.at[me], note_send.at[j], note_recv.at[j])

    def note_arrival(j):
        peer = shifted(me, devices, away[j], -1)
        return copy_to(peer, notes.at[peer], notes_in.at[peer], note_send.at[j], note_recv.at[j])

    first_set, second_set, third_set, last_set = [], [], [], []
    for j, (dz, dy, dc) in enumerate(away):
        if 2 * dz != depth:
            last_set.append(j)
        elif dc == 0:
            first_set.append(j)
        elif dy == 0:
            second_set.append(j)
        else:
            third_set.append(j)

    def fill_all(chosen):
        for j in chosen:
            fill(shifted(me, devices, away[j], 1))

    def start_all(chosen):
        for j in chosen:
            exchange(j).start()

    greet([shifted(me, devices, o, 1) for o in away])
    fetch = pltpu.make_async_copy(weights.at[pl.ds(0, here)], weight, fetch_sem)
    fetch.start()
    for b in range(pairs // NBR):
        feats[b] = feat[:, b * size : (b + 1) * size]
    fill_all(first_set)
    start_all(first_set)

    point_phases(xy, phases)
    count = waves.shape[0] // pairs

    def transform(b, carry):
        values = feats[b]
        for k in range(NBR):
            p = b * NBR + k
            block = jnp.dot(values, kern[p], preferred_element_type=F32).astype(BF16)
            both = lax.dot_general(depths[...], block, NT, preferred_element_type=F32)
            waves[pl.ds(p, count, stride=pairs), :] = jnp.concatenate([both[:count], both[count:]], axis=1)
        return carry

    lax.fori_loop(0, pairs // NBR, transform, 0)
    tall = phases.shape[1]
    lane = 2 * channels
    groups_z, per_group = MZ // here, here // 2
    for w in range(MZ // 2):
        values = waves[w * tall : (w + 1) * tall, :].astype(BF16)
        sums = jnp.dot(phases[...], values, preferred_element_type=F32)
        cols = slice(w % per_group * lane, (w % per_group + 1) * lane)
        for ky in range(MY):
            d = ky * groups_z + w // per_group
            block = sums[ky * 2 * MX : (ky + 1) * 2 * MX, :]
            part[d, :, cols] = block
            part_send[d, :, cols] = block.astype(BF16)

    own = pltpu.make_async_copy(send.at[me], got.at[me], own_sem)

    def filler():
        fill_all(second_set)
        start_all(second_set)
        fill_all(third_set)

    def pushed():
        start_all(third_set)
        fill_all(last_set)
        fill(me)
        own.start()
        notes_in[me] = notes[me]
        fetch.wait()

    modes, sent = reduce_blocks(
        me, depth, part, part_send, from_twin, kept, side_send, from_side, line_send, from_line, sems[:6], filler, pushed
    )

    rows = 2 * MX
    row_wave = lax.broadcasted_iota(jnp.int32, (rows, lane), 0) % MX
    half = lax.broadcasted_iota(jnp.int32, (rows, lane), 1) // channels
    left = half == 0
    fan = MX // 2

    def spread_of(m):
        mine = modes[:, m // 2 * lane : (m // 2 + 1) * lane]
        other = pltpu.roll(mine, channels, 1)
        twice = jnp.where(left, mine, other) if m % 2 == 0 else jnp.where(left, other, mine)
        return jnp.concatenate(
            [jnp.where(row_wave == 2 * f + half, twice, 0.0).astype(BF16) for f in range(fan)], axis=1
        )

    mix_modes(channels, spread_of, weight, mode_scale(me, here, channels), full, me)

    def arrived(i, block):
        if i == 0:
            start_all(last_set)
            for j in range(len(away)):
                note_exchange(j).start()
        spread[block] = jnp.dot(inverse[me], full[block], preferred_element_type=F32)

    sent = sent + gather_blocks(me, depth, full, *sems[6:], arrived)
    back = pltpu.make_async_copy(full, full_out, full_sem)
    back.start()
    lay_lines(channels, planes, here, spread, lines_now, lines_out)
    fill_table(here, table, cos_now, sin_now, cos_step, sin_step)
    put = pltpu.make_async_copy(table, table_out, table_sem)
    put.start()
    for copy in sent:
        copy.wait_send()
    for j in range(len(away)):
        note_exchange(j).wait_send()
        note_arrival(j).wait_recv()
        exchange(j).wait_send()
        arrival(j).wait_recv()
    own.wait()
    back.wait()
    put.wait()


def table_tile(table, k, wide):
    return jnp.concatenate([table[k * wide + i] for i in range(wide)], axis=1)


def place_kernel(cap, channels, per_plane, targets, got, field, send):
    size = got.shape[2]

    def clear(k, carry):
        field[:, pl.ds(pl.multiple_of(k * size, size), size)] = jnp.zeros((field.shape[0], size), F32)
        return carry

    lax.fori_loop(0, field.shape[1] // size, clear, 0)

    def add(d, carry):
        for i in range(cap):
            t = targets[d, 0, i]

            @pl.when(t >= 0)
            def _():
                rows = pl.ds(pl.multiple_of(t // per_plane * channels, channels), channels)
                cols = pl.ds(pl.multiple_of(t % per_plane * size, size), size)
                field[rows, cols] += got[d, i * channels : (i + 1) * channels, :].astype(F32)

        return carry

    lax.fori_loop(0, got.shape[0], add, 0)

    def pick(d, carry):
        for i in range(cap):
            t = jnp.maximum(targets[d, 0, i], 0)
            rows = pl.ds(pl.multiple_of(t // per_plane * channels, channels), channels)
            cols = pl.ds(pl.multiple_of(t % per_plane * size, size), size)
            send[d, i] = field[rows, cols].astype(BF16)
        return carry

    lax.fori_loop(0, got.shape[0], pick, 0)


def pen_position(me):
    return me // 4, me // 2 % 2, me % 2


def greet(partners):
    barrier = pltpu.get_barrier_semaphore()
    for d in partners:
        pl.semaphore_signal(barrier, inc=1, device_id={"pen": d}, device_id_type=MESH)
    pl.semaphore_wait(barrier, len(partners))


def flip(z, mask):
    bit = 1
    while bit <= mask:
        if mask & bit:
            z = z + bit * (1 - 2 * (z // bit % 2))
        bit *= 2
    return z


def at(z, y, c):
    return z * 4 + y * 2 + c


def copy_to(peer, src, dst, send_sem, recv_sem):
    return pltpu.make_async_remote_copy(
        src_ref=src, dst_ref=dst, send_sem=send_sem, recv_sem=recv_sem, device_id={"pen": peer}, device_id_type=MESH
    )


def low_bit(mask):
    return mask & -mask


def reduce_blocks(me, depth, part, part_send, from_twin, kept, side_send, from_side, line_send, from_line, sems, filler, pushed):
    twin_send_sem, twin_recv_sem, side_send_sem, side_recv_sem, line_send_sem, line_recv_sem = sems
    z, y, c = pen_position(me)
    side, twin = at(z, 1 - y, c), at(z, y, 1 - c)
    walk = sorted(range(depth), key=lambda m: (low_bit(m) or depth, m))
    sent = []

    def start(copy):
        copy.start()
        sent.append(copy)
        return copy

    twins, sides, lines = {}, {}, {}
    for m in walk:
        z2 = flip(z, m)
        for f in range(2):
            y2 = (y + 1 + f) % 2
            k = 2 * m + f
            twins[m, f] = start(
                copy_to(twin, part_send.at[at(z2, y2, 1 - c)], from_twin.at[z2 * 2 + y2], twin_send_sem.at[k], twin_recv_sem.at[k])
            )
    filler()
    for m in walk:
        z2 = flip(z, m)
        twins[m, 0].wait_recv()
        side_send[z2] = (part[at(z2, 1 - y, c)] + from_twin[z2 * 2 + 1 - y].astype(F32)).astype(BF16)
        twins[m, 1].wait_recv()
        kept[z2] = part[at(z2, y, c)] + from_twin[z2 * 2 + y].astype(F32)
        sides[m] = start(copy_to(side, side_send.at[z2], from_side.at[z2], side_send_sem.at[m], side_recv_sem.at[m]))

    def push(m):
        line_send[m - 1] = kept[flip(z, m)].astype(BF16)
        peer = at(flip(z, low_bit(m)), y, c)
        lines[m] = start(copy_to(peer, line_send.at[m - 1], from_line.at[m - 1], line_send_sem.at[m - 1], line_recv_sem.at[m - 1]))

    for m in walk:
        z2 = flip(z, m)
        sides[m].wait_recv()
        kept[z2] = kept[z2] + from_side[z2].astype(F32)
        if m % 2:
            push(m)
    stride = 1
    while stride < depth:
        for m in range(1, depth):
            if low_bit(m) == stride:
                lines[m].wait_recv()
                z2 = flip(z, m - stride)
                kept[z2] = kept[z2] + from_line[m - 1].astype(F32)
        stride *= 2
        for m in range(1, depth):
            if low_bit(m) == stride:
                push(m)
        if 2 * stride == depth:
            pushed()
    return kept[z], sent


def gather_blocks(me, depth, full, z_send, z_recv, y_send, y_recv, c_send, c_recv, arrived):
    z, y, c = pen_position(me)
    side, twin = at(z, 1 - y, c), at(z, y, 1 - c)
    strides = [depth >> (i + 1) for i in range(depth.bit_length() - 1)]
    started = []

    def push(block, target, send_sem, recv_sem):
        copy = copy_to(target, full.at[block], full.at[block], send_sem, recv_sem)
        copy.start()
        started.append(copy)

    def landed(block, send_sem, recv_sem):
        copy_to(twin, full.at[block], full.at[block], send_sem, recv_sem).wait_recv()

    def mask_of(i):
        return sum(strides[b] for b in range(len(strides)) if i >> b & 1)

    def onward(i, level):
        block = at(flip(z, mask_of(i)), y, c)
        for deeper in range(level, len(strides)):
            k = (1 << deeper) + i - 1
            push(block, at(flip(z, strides[deeper]), y, c), z_send.at[k], z_recv.at[k])
        push(block, side, y_send.at[i], y_recv.at[i])
        push(block, twin, c_send.at[i], c_recv.at[i])
        arrived(i, block)

    onward(0, 0)
    for i in range(1, depth):
        landed(at(flip(z, mask_of(i)), y, c), z_send.at[i - 1], z_recv.at[i - 1])
        onward(i, i.bit_length())
    for i in range(depth):
        block = at(flip(z, mask_of(i)), 1 - y, c)
        landed(block, y_send.at[i], y_recv.at[i])
        push(block, twin, c_send.at[depth + i], c_recv.at[depth + i])
        arrived(depth + i, block)
    for i in range(2 * depth):
        block = at(flip(z, mask_of(i % depth)), y if i < depth else 1 - y, 1 - c)
        landed(block, c_send.at[i], c_recv.at[i])
        arrived(2 * depth + i, block)
    return started


def mix_modes(channels, spread_of, weight, scaling, full, me):
    rows = 2 * MX
    width = 2 * channels
    left = lax.broadcasted_iota(jnp.int32, (rows, width), 1) < channels
    for pair in range(weight.shape[0] // 2):
        halves = []
        for k in range(2):
            prod = jnp.dot(spread_of(2 * pair + k), weight[2 * pair + k], preferred_element_type=F32)
            real, imag = prod[:MX], prod[MX:]
            real_turned = pltpu.roll(real, channels, 1)
            imag_turned = pltpu.roll(imag, channels, 1)
            if k == 0:
                halves.append((real - imag_turned, real_turned + imag))
            else:
                halves.append((real_turned - imag, real + imag_turned))
        (real_a, imag_a), (real_b, imag_b) = halves
        top = left[:MX]
        both = jnp.concatenate([jnp.where(top, real_a, real_b), jnp.where(top, imag_a, imag_b)], axis=0)
        both = (both * scaling[:, pair * width : (pair + 1) * width]).astype(BF16)
        full[me, :, pair * width : (pair + 1) * width] = both


def mode_scale(me, here, channels):
    cell = lax.broadcasted_iota(jnp.int32, (1, here * channels), 1)
    wave_z = lax.rem(me * here + lax.div(cell, channels), MZ)
    return jnp.where(wave_z == 0, 1.0, 2.0) * (1.0 / (NX * NY * NZ))


def gelu_twice(v):
    scale = math.sqrt(2.0 / math.pi)
    turn = jnp.tanh(v * (BF16(scale) + BF16(scale * 0.044715) * (v * v)))
    return v + v * turn


def local_rows(planes, channels):
    waves = np.arange(MX) - MX // 2
    angle = 2 * np.pi * np.mod(np.outer(np.arange(planes), waves), NX) / NX
    quarter = MX // 4
    both = np.stack([np.cos(angle).reshape(planes, 4, quarter), np.sin(angle).reshape(planes, 4, quarter)], axis=2)
    return jnp.asarray(np.repeat(both.reshape(planes, 4, 2 * quarter), channels, axis=2).transpose(1, 0, 2), F32)


def fill_local(channels, rows, local):
    lanes = rows.shape[2]
    same = lax.broadcasted_iota(jnp.int32, (channels, lanes), 0) == lax.broadcasted_iota(jnp.int32, (channels, lanes), 1) % channels
    for q in range(rows.shape[0]):
        for p in range(rows.shape[1]):
            local[q, p * channels : (p + 1) * channels, :] = jnp.where(same, rows[q, p : p + 1, :], 0.0).astype(BF16)


def turn_table(devices, channels):
    waves = np.arange(MX) - MX // 2
    angle = 2 * np.pi * np.mod(np.outer(np.arange(devices) * (NX // devices), waves), NX) / NX
    parts = np.stack([np.cos(angle), np.sin(angle)], axis=1)
    return jnp.asarray(np.repeat(parts, channels, axis=2), F32)


def along_parts(spec, local, turns, me, here, part, part_send):
    devices = part.shape[0]
    values = spec[...].astype(BF16)
    for q in range(local.shape[0]):
        prod = jnp.dot(values, local[q], preferred_element_type=F32)
        width = prod.shape[1] // 2
        cols = slice(q * width, (q + 1) * width)
        cos, sin = turns[me, 0:1, cols], turns[me, 1:2, cols]
        for d in range(devices):
            base = d * 2 * here
            real_rows, imag_rows = prod[base : base + here], prod[base + here : base + 2 * here]
            own_real = real_rows[:, :width] + imag_rows[:, width:]
            own_imag = imag_rows[:, :width] - real_rows[:, width:]
            block = jnp.concatenate([own_real * cos + own_imag * sin, own_imag * cos - own_real * sin], axis=0)
            part[d, :, cols] = block
            part_send[d, :, cols] = block.astype(BF16)


def offsets(devices):
    return [(dz, dy, dc) for dz in range(devices // 4) for dy in range(2) for dc in range(2) if dz + dy + dc]


def shifted(me, devices, offset, sign):
    z, y, c = pen_position(me)
    dz, dy, dc = offset
    depth = devices // 4
    return (z + (dz if sign > 0 else depth - dz)) % depth * 4 + (y + dy) % 2 * 2 + (c + dc) % 2


def wide_gelu_twice(v):
    scale = math.sqrt(2.0 / math.pi)
    turn = jnp.tanh(v * (scale + scale * 0.044715 * (v * v)))
    return (v + v * turn).astype(BF16)


def make_waves(turned, full, waves, number, channels):
    tall, lane = turned.shape[0], 2 * channels
    devices = full.shape[0]
    groups_z = devices // MY
    per_group = full.shape[2] // lane
    for w in range(MZ // 2):
        g, cols = w // per_group, slice(w % per_group * lane, (w % per_group + 1) * lane)
        rows = jnp.concatenate([full[ky * groups_z + g, :, cols] for ky in range(MY)], axis=0)
        waves[number, w * tall : (w + 1) * tall, :] = jnp.dot(turned[...], rows, preferred_element_type=F32)


def layer_kernel(
    devices, planes, wide, cap,
    slot_of, modes, table, field, ups, downs, local_small, turns, depths, slots_xy, picked, weights, first_in, kern_in,
    answer,
    total, summed, out, part, part_send, from_twin, kept, side_send, from_side, line_send, from_line,
    weight, first, second, local, fetched, kern, phases, turned, waves, results, up, down,
    own_sem, fetch_sem, first_sem, kern_sem, send_sem, recv_sem, *sems,
):
    channels = field.shape[0] // planes
    here = weight.shape[0]
    size = kern.shape[1]
    pairs = kern.shape[0]
    me = lax.axis_index("pen")
    step, steps = pl.program_id(0), pl.num_programs(0)
    order = offsets(devices)
    depth = devices // 4

    def exchange(j):
        peer = shifted(me, devices, order[j], 1)
        return copy_to(peer, picked.at[peer], fetched.at[me], send_sem.at[j], recv_sem.at[j])

    early, second_set, third_set, last_set = [], [], [], []
    for j, (dz, dy, dc) in enumerate(order):
        if 2 * dz < depth or (2 * dz > depth and dc == 0):
            early.append(j)
        elif 2 * dz > depth or (dy == 0 and dc == 0):
            second_set.append(j)
        elif dc == 0:
            third_set.append(j)
        else:
            last_set.append(j)

    def start_all(chosen):
        for j in chosen:
            exchange(j).start()

    own = pltpu.make_async_copy(picked.at[me], fetched.at[me], own_sem)
    fetch = pltpu.make_async_copy(weights.at[pl.ds(here, here)], weight, fetch_sem)
    fetch_first = pltpu.make_async_copy(first_in, first, first_sem)
    fetch_kern = pltpu.make_async_copy(kern_in, kern, kern_sem)

    @pl.when(step == 0)
    def _():
        greet([shifted(me, devices, o, 1) for o in order])
        start_all(early)
        own.start()
        fetch.start()
        fetch_first.start()
        fetch_kern.start()
        total[...] = jnp.zeros_like(total)
        for n in range(LAYERS):
            up[n] = ups[n].T
            down[n] = (downs[n].astype(F32) * 0.5).astype(BF16)
        fill_local(channels, local_small, local)
        point_phases(slots_xy, phases)

    tile = table_tile(table, 0, wide)
    summed[...] = field[...] + jnp.dot(modes[...], tile, preferred_element_type=F32)

    def raise_up(p):
        values = summed[p * channels : (p + 1) * channels, :]
        return jnp.dot(up[0], values.astype(BF16), preferred_element_type=F32).astype(BF16)

    ahead = raise_up(0)
    for p in range(planes):
        v = ahead
        if p + 1 < planes:
            ahead = raise_up(p + 1)
        rows = slice(p * channels, (p + 1) * channels)
        values = summed[rows, :] + jnp.dot(down[0], gelu_twice(v), preferred_element_type=F32)
        out[rows, :] = values.astype(BF16)
    total[...] += lax.dot_general(tile, out[...], NT, preferred_element_type=F32)

    @pl.when(step == steps - 1)
    def _():
        start_all(second_set)
        along_parts(total, local, turns, me, here, part, part_send)

        def filler():
            fetch_first.wait()
            turned[...] = phases[...].T
            make_waves(turned, first, waves, 0, channels)

        def pushed():
            start_all(third_set)
            fetch.wait()
            own.wait()
            fetch_kern.wait()

        spectrum, sent = reduce_blocks(
            me, depth, part, part_send, from_twin, kept, side_send, from_side, line_send, from_line, sems[:6], filler, pushed
        )
        lanes = MX * channels
        keep = lax.broadcasted_iota(jnp.int32, (MX, lanes), 0) == lax.broadcasted_iota(jnp.int32, (MX, lanes), 1) // channels

        def spread_of(m):
            top = jnp.where(keep, spectrum[m : m + 1, :], 0.0).astype(BF16)
            low = jnp.where(keep, spectrum[here + m : here + m + 1, :], 0.0).astype(BF16)
            return jnp.concatenate([top, low], axis=0)

        mix_modes(channels, spread_of, weight, mode_scale(me, here, channels), second, me)

        def arrived(i, block):
            if i == 0:
                start_all(last_set)

        sent = sent + gather_blocks(me, depth, second, *sems[6:], arrived)
        make_waves(turned, second, waves, 1, channels)
        slots = devices * cap
        count = waves.shape[1] // slots

        def spectral(number, slot):
            value = waves[number, pl.ds(slot, count, stride=slots), :].astype(BF16)
            both = lax.dot_general(value, depths[...], TN, preferred_element_type=F32)
            return both[:channels, :size] + both[channels:, size:]

        def finish(peer):
            values = jnp.concatenate([fetched[peer, i].astype(F32) for i in range(cap)], axis=1)
            for n in range(LAYERS):
                now = values + jnp.concatenate([spectral(n, peer * cap + i) for i in range(cap)], axis=1)
                v = jnp.dot(up[n], now.astype(BF16), preferred_element_type=F32)
                values = now + jnp.dot(down[n], wide_gelu_twice(v), preferred_element_type=F32)
            values = values.astype(BF16)
            for i in range(cap):
                results[peer * cap + i] = values[:, i * size : (i + 1) * size]

        def take(t, carry):
            peer = shifted(me, devices, (t // 4, t // 2 % 2, t % 2), -1)

            @pl.when(t > 0)
            def _():
                copy_to(peer, picked.at[peer], fetched.at[peer], send_sem.at[t - 1], recv_sem.at[t - 1]).wait_recv()

            finish(peer)
            return carry

        middle = depth // 2
        lax.fori_loop(0, 4 * middle, take, 0)
        beyond = 2 * (depth - middle - 1)
        lax.fori_loop(0, 2 * beyond, lambda i, carry: take(4 * (middle + 1) + i % beyond * 2 + i // beyond, carry), 0)
        lax.fori_loop(0, 4, lambda i, carry: take(4 * middle + i % 2 * 2 + i // 2, carry), 0)

        def project(b, carry):
            acc = None
            for k in range(NBR):
                p = b * NBR + k
                term = lax.dot_general(results[slot_of[p]], kern[p], NT, preferred_element_type=F32)
                acc = term if acc is None else acc + term
            answer[:, pl.ds(pl.multiple_of(b * size, size), size)] = acc
            return carry

        lax.fori_loop(0, pairs // NBR, project, 0)
        for copy in sent:
            copy.wait_send()
        for j in range(len(order)):
            exchange(j).wait_send()


def depth_table(size):
    lines_here = size // NZ
    wave = np.arange(MZ)
    cell = np.arange(size)
    angle = 2 * np.pi * np.mod(np.outer(wave, cell % NZ), NZ) / NZ
    on_line = (cell // NZ)[None, :] == np.arange(lines_here)[:, None]
    parts = np.stack([np.cos(angle), -np.sin(angle)], axis=1)
    full = parts[:, :, None, :] * on_line[None, None, :, :]
    full = full.reshape(MZ // 2, 2, 2 * lines_here, size).transpose(0, 2, 1, 3)
    return jnp.asarray(full.reshape(MZ // 2 * 2 * lines_here, 2 * size), BF16)


def plane_inverse(devices):
    planes = NX // devices
    waves = np.arange(MX) - MX // 2
    angle = 2 * np.pi * np.mod(np.outer(np.arange(NX), waves), NX) / NX
    cos, sin = np.cos(angle).reshape(devices, planes, MX), np.sin(angle).reshape(devices, planes, MX)
    real = np.concatenate([cos, -sin], axis=2)
    imag = np.concatenate([sin, cos], axis=2)
    return jnp.asarray(np.concatenate([real, imag], axis=1), BF16)


def per_device(point_feat, pair_kernel, pair_owner, pair_block, spec_weight, mlp_up, mlp_down):
    devices = lax.axis_size("pen")
    pairs, size = pair_kernel.shape[0], pair_kernel.shape[1]
    channels = point_feat.shape[0]
    cap = 2 * pairs // devices
    planes = NX // devices
    plane_cells = NY * NZ
    per_plane = plane_cells // size
    here = spec_weight.shape[1]
    modes_all = MY * MZ
    lines = planes * channels
    wide = 4
    lines_here = size // NZ
    depth = devices // 4
    peers = devices - 1
    waves_tall = 2 * lines_here * pairs
    DMA = pltpu.SemaphoreType.DMA
    shape = jax.ShapeDtypeStruct
    weights = spec_weight.reshape(LAYERS * here, MX * channels, 2 * channels)
    depths = depth_table(size)
    depth_rows = depths.shape[0]
    forward_depths = depths.reshape(depth_rows, 2, size).transpose(1, 0, 2).reshape(2 * depth_rows, size)
    owner = pair_owner[:, 0]

    order, source, slot_of, notes, xy, slots_xy = pl.pallas_call(
        functools.partial(lists_kernel, devices, cap, planes, per_plane, lines_here),
        out_shape=(
            shape((devices * cap,), jnp.int32),
            shape((devices * cap,), jnp.int32),
            shape((pairs,), jnp.int32),
            shape((devices, 8, 128), jnp.int32),
            shape((2, lines_here * pairs), jnp.int32),
            shape((2, lines_here * devices * cap), jnp.int32),
        ),
        in_specs=[SMEM, SMEM, VMEM, VMEM],
        out_specs=(SMEM, SMEM, SMEM, VMEM, VMEM, VMEM),
        scratch_shapes=[pltpu.SMEM((devices * cap,), jnp.int32), pltpu.SMEM((devices,), jnp.int32)],
        name="lists",
    )(owner, pair_block, owner.reshape(1, pairs), pair_block.reshape(1, pairs))

    gather_sems = [DMA((depth - 1,)), DMA((depth - 1,)), DMA((depth,)), DMA((depth,)), DMA((2 * depth,)), DMA((2 * depth,))]
    full_shape = (devices, 2 * MX, here * channels)
    weight_shape = (here, MX * channels, 2 * channels)
    table_shape = (plane_cells // size, 2 * modes_all, size)
    block_shape = full_shape[1:]
    trig = pltpu.VMEM((2 * modes_all, size), F32)
    reduce_scratch = [
        pltpu.VMEM((2 * depth,) + block_shape, BF16),
        pltpu.VMEM((depth,) + block_shape, F32),
        pltpu.VMEM((depth,) + block_shape, BF16),
        pltpu.VMEM((depth,) + block_shape, BF16),
        pltpu.VMEM((depth - 1,) + block_shape, BF16),
        pltpu.VMEM((depth - 1,) + block_shape, BF16),
    ]
    reduce_sems = [DMA((2 * depth,)), DMA((2 * depth,)), DMA((depth,)), DMA((depth,)), DMA((depth - 1,)), DMA((depth - 1,))]
    got, wanted, first, modes, table = pl.pallas_call(
        functools.partial(encode_kernel, devices, cap, planes),
        out_shape=(
            shape((devices, cap * channels, size), BF16),
            shape((devices, 8, 128), jnp.int32),
            shape(full_shape, BF16),
            shape((lines, 2 * modes_all), BF16),
            shape(table_shape, BF16),
        ),
        in_specs=[SMEM] * 2 + [VMEM] * 6 + [ANY],
        out_specs=(ANY, VMEM, ANY, VMEM, ANY),
        scratch_shapes=[
            pltpu.VMEM((MY * 2 * MX, waves_tall), BF16),
            pltpu.VMEM((pairs // NBR, channels, size), BF16),
            pltpu.VMEM((devices, cap * channels, size), BF16),
            pltpu.VMEM((MZ // 2 * waves_tall, 2 * channels), F32),
            pltpu.VMEM(full_shape, F32),
            pltpu.VMEM(full_shape, BF16),
        ]
        + reduce_scratch
        + [
            pltpu.VMEM(weight_shape, BF16),
            pltpu.VMEM(full_shape, BF16),
            pltpu.VMEM((devices, 2 * planes, here * channels), F32),
            pltpu.VMEM((2 * modes_all, lines), F32),
            pltpu.VMEM(table_shape, BF16),
            trig,
            trig,
            trig,
            trig,
            DMA,
            DMA,
            DMA,
            DMA,
            DMA((peers,)),
            DMA((peers,)),
            DMA((peers,)),
            DMA((peers,)),
        ]
        + reduce_sems
        + gather_sems,
        compiler_params=pltpu.CompilerParams(collective_id=0, has_side_effects=True),
        name="encode",
    )(order, source, notes, xy, point_feat, pair_kernel, forward_depths, plane_inverse(devices), weights)

    field, picked = pl.pallas_call(
        functools.partial(place_kernel, cap, channels, per_plane),
        out_shape=(shape((lines, plane_cells), F32), shape((devices, cap, channels, size), BF16)),
        in_specs=[SMEM, VMEM],
        out_specs=(VMEM, VMEM),
        name="place",
    )(wanted, got)

    chunk = wide * size
    local_small = local_rows(planes, channels)
    turns = turn_table(devices, channels)
    whole = lambda extent: pl.BlockSpec(extent, lambda k: (0,) * len(extent))
    slots = devices * cap
    part_shape = (devices, 2 * here, MX * channels)
    line_shape = part_shape[1:]
    return pl.pallas_call(
        functools.partial(layer_kernel, devices, planes, wide, cap),
        out_shape=shape((channels, pairs // NBR * size), F32),
        grid=(plane_cells // chunk,),
        in_specs=[
            SMEM,
            whole((lines, 2 * modes_all)),
            pl.BlockSpec((wide, 2 * modes_all, size), lambda k: (k, 0, 0)),
            pl.BlockSpec((lines, chunk), lambda k: (0, k)),
            whole((LAYERS,) + mlp_up.shape[:0:-1]),
            whole(mlp_down.shape),
            whole(local_small.shape),
            whole(turns.shape),
            whole(depths.shape),
            whole(slots_xy.shape),
            ANY,
            ANY,
            ANY,
            ANY,
        ],
        out_specs=whole((channels, pairs // NBR * size)),
        scratch_shapes=[
            pltpu.VMEM((2 * modes_all, lines), F32),
            pltpu.VMEM((lines, chunk), F32),
            pltpu.VMEM((lines, chunk), BF16),
            pltpu.VMEM(part_shape, F32),
            pltpu.VMEM(part_shape, BF16),
            pltpu.VMEM((2 * depth,) + line_shape, BF16),
            pltpu.VMEM((depth,) + line_shape, F32),
            pltpu.VMEM((depth,) + line_shape, BF16),
            pltpu.VMEM((depth,) + line_shape, BF16),
            pltpu.VMEM((depth - 1,) + line_shape, BF16),
            pltpu.VMEM((depth - 1,) + line_shape, BF16),
            pltpu.VMEM(weight_shape, BF16),
            pltpu.VMEM(full_shape, BF16),
            pltpu.VMEM(full_shape, BF16),
            pltpu.VMEM((local_small.shape[0], lines, local_small.shape[2]), BF16),
            pltpu.VMEM((devices, cap, channels, size), BF16),
            pltpu.VMEM(pair_kernel.shape, BF16),
            pltpu.VMEM((MY * 2 * MX, 2 * lines_here * slots), BF16),
            pltpu.VMEM((2 * lines_here * slots, MY * 2 * MX), BF16),
            pltpu.VMEM((LAYERS, MZ // 2 * 2 * lines_here * slots, 2 * channels), F32),
            pltpu.VMEM((slots, channels, size), BF16),
            pltpu.VMEM(mlp_up.shape, BF16),
            pltpu.VMEM(mlp_down.shape, BF16),
            DMA,
            DMA,
            DMA,
            DMA,
            DMA((peers,)),
            DMA((peers,)),
        ]
        + reduce_sems
        + gather_sems,
        compiler_params=pltpu.CompilerParams(collective_id=1, has_side_effects=True),
        name="layer",
    )(slot_of, modes, table, field, mlp_up.transpose(0, 2, 1), mlp_down, local_small, turns, depths, slots_xy, picked, weights, first, pair_kernel)


def solution(mesh):
    in_specs = (
        P(None, ("groups", "pen")),
        P(("groups", "pen"), None, None),
        P(("groups", "pen"), None),
        P(("groups", "pen")),
        P(None, "pen", None, None, None),
        P(),
        P(),
    )
    out_specs = P(None, ("groups", "pen"))
    return jax.shard_map(
        per_device, mesh=mesh, in_specs=in_specs, out_specs=out_specs, check_vma=False
    )
```
